32 devices in a mesh: parts: 2 (over y), leaf: 4 (over z), sub: 4 (over x, core).
Axes of the slice: x: 2, y: 2, z: 4, core: 2. Of those that a mesh axis runs over, the one named last changes fastest.
Arguments:
- points: float32 [6, 65536], P(None, ('parts', 'leaf', 'sub')), parts along dimension 1
- targets: float32 [64, 65536], P(None, ('parts', 'leaf', 'sub')), parts along dimension 1
- leaf_skel: int32 [32, 256], P(('parts', 'leaf', 'sub')), parts along dimension 0, may hold values from 0 to 2047, as said below
- node_keep: int32 [30, 256], P('parts'), parts along dimension 0, may hold values from 0 to 511, as said below
- lengthscales: float32 [12], P('parts'), parts along dimension 0, may hold values from 0.25 to 0.35
- noise_var: float32 [2], P('parts'), parts along dimension 0, may hold values from 0.5 to 1.5
Outputs:
- solution: float32 [64, 65536], P(None, ('parts', 'leaf', 'sub')), parts along dimension 1
- residual: float32 [64, 65536], P(None, ('parts', 'leaf', 'sub')), parts along dimension 1
The draws below stay inside these ranges and needn't reach their ends.
There are 2 independent parts, one for each index of `parts`. The reference program is written for one: setup_inputs(seed, part) draws one part's arguments, and reference() takes and returns one part's arrays. A program takes and returns all parts, laid end to end along the dimension named above; each array names one. Nothing has to cross between parts.
Inputs may be any that keep to these rules, and one draw needn't show every extreme that they name: `leaf_skel`: row t lists 256 distinct positions among the 2048 points of leaf t. `node_keep`: row n lists 256 distinct positions in the concatenation of the skeletons of heap nodes 2n+1 and 2n+2, the first node's 256 points before the second's.
All inputs are finite; a program needn't handle non-finite values.
Results may differ from the reference program's by a relative error of at most 0.0004.
Values sent between devices are 32-bit elements; how exact they have to be, the bound alone decides.
No kernel may reach another device: no remote copies, remote signals or barrier semaphores. Data moves between devices by JAX's collectives and lax.ppermute only.
A program may use at most 128 MiB of HBM per device.

```python
import math
import jax
import jax.numpy as jnp
from jax import lax

DIMS = 6
LEAF = 2048
RANK = 256
RHS = 64
ITERS = 3
LEVELS = 4
LEAVES = 16
NODES = 15
POINTS = 32768


def draw_points(key, part):
    position = jnp.arange(POINTS, dtype=jnp.int32)
    leaf_number = position // LEAF
    spread = jax.random.uniform(key, (DIMS, POINTS), jnp.float32)
    region = 2.4
    coordinate_rows = []
    for axis_number in range(DIMS):
        corner = jnp.zeros((POINTS,), jnp.float32)
        extent = 1.0
        for tree_depth in range(LEVELS):
            if tree_depth % DIMS == axis_number:
                extent = 0.5
                bit_value = (leaf_number >> LEVELS - 1 - tree_depth & 1).astype(jnp.float32)
                corner = bit_value * extent
        coordinate_rows.append(region * (0.2 * corner + spread[axis_number]))
    return jnp.stack(coordinate_rows)


def draw_targets(key, part):
    ramp = 1.0 + 2.0 * jnp.arange(POINTS, dtype=jnp.float32) / POINTS
    values = jax.random.normal(key, (RHS, POINTS), jnp.float32)
    return values * ramp[None, :]


def rotated_picks(key, rows, pool, picks):
    keys = jax.random.split(key, rows)
    chosen = jax.vmap(lambda one_key: jax.random.permutation(one_key, pool)[:picks])(keys)
    row_number = jnp.arange(rows, dtype=jnp.int32)
    target_value = jnp.where(row_number % 2 == 0, pool - 1, 0)
    moved = (chosen + (target_value - chosen[:, 0])[:, None] + pool) % pool
    return moved.astype(jnp.int32)


def draw_leaf_skel(key, part):
    return rotated_picks(jax.random.fold_in(key, 11), LEAVES, LEAF, RANK)


def draw_node_keep(key, part):
    return rotated_picks(jax.random.fold_in(key, 23), NODES, 2 * RANK, RANK)


def setup_inputs(seed: int = 0, part: int = 0) -> dict:
    splits = jax.random.split(jax.random.key(seed), 7)
    own_keys = jax.random.split(jax.random.fold_in(splits[6], part), 7)
    return {
        "points": draw_points(jax.random.fold_in(jax.random.fold_in(splits[6], part), 71), part),
        "targets": draw_targets(jax.random.fold_in(jax.random.fold_in(splits[6], part), 71), part),
        "leaf_skel": draw_leaf_skel(jax.random.fold_in(jax.random.fold_in(splits[6], part), 71), part),
        "node_keep": draw_node_keep(jax.random.fold_in(jax.random.fold_in(splits[6], part), 71), part),
        "lengthscales": jnp.clip(jnp.exp(jax.random.uniform(own_keys[4], (DIMS,), jnp.float32, math.log(0.25), math.log(0.35))), 0.25, 0.35),
        "noise_var": jnp.clip(jax.random.uniform(own_keys[5], (1,), jnp.float32, 0.5, 1.5), 0.5, 1.5),
    }


def kernel(left, right, inverse_scale):
    squared = jnp.zeros((left.shape[1], right.shape[1]), jnp.float32)
    for axis_number in range(left.shape[0]):
        offset = (left[axis_number][:, None] - right[axis_number][None, :]) * inverse_scale[axis_number]
        squared = squared + offset * offset
    return jnp.exp(-0.5 * squared)


def product(first, second):
    return jnp.dot(first, second, precision=lax.Precision.HIGHEST, preferred_element_type=jnp.float32)


def batch_stacked_rows(form, first, second):
    return jnp.einsum(form, first.astype(jnp.float32), second.astype(jnp.float32), precision=lax.Precision.HIGHEST)


def exchange_pairs(stacked):
    shape = stacked.shape
    return stacked.reshape((shape[0] // 2, 2) + shape[1:])[:, ::-1].reshape(shape)


def reference(points, targets, leaf_skel, node_keep, lengthscales, noise_var):
    inverse_scale = 1.0 / lengthscales
    leaf_points = points.reshape(DIMS, LEAVES, LEAF).transpose(1, 0, 2)
    skeletons = jnp.take_along_axis(leaf_points, leaf_skel[:, None, :], axis=2)
    coords = [skeletons]
    transfer_matrices = []
    cross_edge_list = []
    for tree_level in range(1, LEVELS + 1):
        child = coords[-1]
        cross_edge_list.append(lax.map(lambda pieces: kernel(pieces[0], pieces[1], inverse_scale), (exchange_pairs(child), child)))
        joined = jnp.concatenate([child[0::2], child[1::2]], axis=2)
        node_count = joined.shape[0]
        first_node = (1 << (LEVELS - tree_level)) - 1
        chosen = node_keep[first_node:first_node + node_count]
        parents = jnp.take_along_axis(joined, chosen[:, None, :], axis=2)
        transfer_matrices.append(lax.map(lambda pieces: kernel(pieces[0], pieces[1], inverse_scale), (joined, parents)))
        coords.append(parents)

    def apply_operator(values):
        by_leaf = values.reshape(RHS, LEAVES, LEAF).transpose(1, 0, 2)

        def leaf_upward(pieces):
            return product(pieces[2], kernel(pieces[0], pieces[1], inverse_scale))

        node_weight = lax.map(leaf_upward, (leaf_points, skeletons, by_leaf))
        upward_weight = [node_weight]
        for tree_level in range(1, LEVELS + 1):
            joined_weight_block = jnp.concatenate([node_weight[0::2], node_weight[1::2]], axis=2)
            node_weight = batch_stacked_rows("uht,utk->uhk", joined_weight_block, transfer_matrices[tree_level - 1])
            upward_weight.append(node_weight)
        search_vector = jnp.zeros((1, RHS, RANK), jnp.float32)
        for tree_level in range(LEVELS, 0, -1):
            downward_sweep = batch_stacked_rows("ckp,cip->cki", search_vector, transfer_matrices[tree_level - 1])
            half_pieces = jnp.stack([downward_sweep[:, :, :RANK], downward_sweep[:, :, RANK:]], axis=1)
            half_pieces = half_pieces.reshape(-1, RHS, RANK)
            search_vector = batch_stacked_rows("uht,utk->uhk", exchange_pairs(upward_weight[tree_level - 1]), cross_edge_list[tree_level - 1]) + half_pieces

        def leaf_output(pieces):
            leaf_coords, leaf_skeleton, leaf_values, leaf_z = pieces
            near_term = product(leaf_values, kernel(leaf_coords, leaf_coords, inverse_scale))
            far_term = product(leaf_z, kernel(leaf_skeleton, leaf_coords, inverse_scale))
            return near_term + far_term

        outputs = lax.map(leaf_output, (leaf_points, skeletons, by_leaf, search_vector))
        return noise_var[0] * values + outputs.transpose(1, 0, 2).reshape(RHS, POINTS)

    solution = jnp.zeros_like(targets)
    residual = targets
    direction = targets
    norm_now = jnp.sum(residual * residual, axis=1)
    for iteration in range(ITERS):
        image = apply_operator(direction)
        curve = jnp.sum(direction * image, axis=1)
        step_size = norm_now / curve
        solution = solution + step_size[:, None] * direction
        residual = residual - step_size[:, None] * image
        norm_next = jnp.sum(residual * residual, axis=1)
        direction = residual + (norm_next / norm_now)[:, None] * direction
        norm_now = norm_next
    return solution, residual
```

```python
import functools
import math

import jax
import jax.numpy as jnp
from jax import lax
from jax.experimental import pallas as pl
from jax.experimental.pallas import tpu as pltpu
from jax.sharding import PartitionSpec as P

F32 = jnp.float32
BF16 = jnp.bfloat16
VMEM = pl.BlockSpec(memory_space=pltpu.VMEM)
ANY = pl.BlockSpec(memory_space=pl.ANY)
NN = (((1,), (0,)), ((), ()))
NT = (((1,), (1,)), ((), ()))
SCALE = math.sqrt(0.5 * math.log2(math.e))
STRIP = 128
BLOCK = 256


def call(kernel, out_shape, args, anywhere=(), scratch=(), name=None, cost=None):
    total = sum(a.size * a.dtype.itemsize for i, a in enumerate(args) if i not in anywhere)
    total += sum(math.prod(s.shape) * s.dtype.itemsize for s in out_shape)
    if cost is not None:
        cost = pl.CostEstimate(flops=cost[0], transcendentals=cost[1], bytes_accessed=total)
    results = pl.pallas_call(
        kernel,
        out_shape=list(out_shape),
        in_specs=[ANY if i in anywhere else VMEM for i in range(len(args))],
        out_specs=[VMEM] * len(out_shape),
        scratch_shapes=list(scratch),
        compiler_params=pltpu.CompilerParams(vmem_limit_bytes=total + (8 << 20)),
        cost_estimate=cost,
        name=name,
    )(*args)
    return list(results)


def f32_shape(*shape):
    return jax.ShapeDtypeStruct(shape, F32)


def bf16_shape(*shape):
    return jax.ShapeDtypeStruct(shape, BF16)


def split(value):
    high = value.astype(BF16)
    return high, (value - high.astype(F32)).astype(BF16)


def split3(value):
    high = value.astype(BF16)
    rest = value - high.astype(F32)
    middle = rest.astype(BF16)
    return high, middle, (rest - middle.astype(F32)).astype(BF16)


def dot3(value, high, low, dims=NN):
    rows = value.shape[0]
    vh, vl = split(value)
    both = lax.dot_general(
        jnp.concatenate([vh, vl], axis=0), high, dims, preferred_element_type=F32
    )
    return both[:rows] + both[rows:] + lax.dot_general(vh, low, dims, preferred_element_type=F32)


def gauss(left, right, dims):
    squared = None
    for d in range(dims):
        offset = left[:, d : d + 1] - right[d : d + 1, :]
        squared = offset * offset if squared is None else squared + offset * offset
    return jnp.exp2(-squared)


def pick(table, chosen):
    rows, pool = table.shape
    hit = lax.broadcasted_iota(jnp.int32, (pool, chosen.shape[1]), 0) == chosen
    onehot = jnp.where(hit, 1.0, 0.0).astype(BF16)
    parts = [lax.dot_general(t, onehot, NN, preferred_element_type=F32) for t in split3(table)]
    return parts[0] + parts[1] + parts[2]


def to_rows(columns, width):
    rows = columns[0].shape[0]
    lane = lax.broadcasted_iota(jnp.int32, (rows, 128), 1)
    block = jnp.zeros((rows, 128), F32)
    for i, column in enumerate(columns):
        block = jnp.where(lane == i, column, block)
    if rows < 128:
        block = jnp.concatenate([block, jnp.zeros((128 - rows, 128), F32)], axis=0)
    flipped = block.T[:8]
    return jnp.concatenate([flipped, jnp.zeros((8, width - 128), F32)], axis=1)


def to_columns(block, rows):
    square = jnp.concatenate([block[:, :128], jnp.zeros((120, 128), F32)], axis=0)
    return square.T[:rows]


def row_sum(value):
    return jnp.sum(value, axis=1, keepdims=True)


def setup_kernel(stages, total, anchors, *refs):
    sources, refs = refs[:6], refs[6:]
    message, rhs, pts_row, basis_h, basis_l, chosen_out, params = refs[:7]
    pts, skel, keep, scales, noise, pts_col, sems = refs[7:]
    targets = (pts, rhs, skel, keep, scales, noise)
    copies = [
        pltpu.make_async_copy(source, target, sems.at[i])
        for i, (source, target) in enumerate(zip(sources, targets))
    ]
    for copy in copies:
        copy.start()
    for i in (0, 2, 4):
        copies[i].wait()
    dims, count = pts.shape
    points = jnp.concatenate([pts[...], jnp.zeros((8 - dims, count), F32)], axis=0)
    row = lax.broadcasted_iota(jnp.int32, (8, dims), 0)
    lane = lax.broadcasted_iota(jnp.int32, (8, dims), 1)
    spread = jnp.broadcast_to(scales[...], (8, dims))
    length = row_sum(jnp.where(row == lane, spread, 0.0))
    valid = lax.broadcasted_iota(jnp.int32, (8, 1), 0) < dims
    inverse = SCALE / jnp.where(valid, length, 1.0)
    shift = points[:, 0:1]
    chosen = pick(points, skel[...])
    rows = rhs.shape[0]
    message[rows + 8 :, :] = chosen
    scaled = (points - shift) * inverse
    own = (chosen - shift) * inverse
    pts_row[...] = scaled
    pts_col[...] = scaled.T
    for i in range(count // STRIP):
        strip = slice(i * STRIP, (i + 1) * STRIP)
        high, low = split(gauss(pts_col[strip, :], own, dims))
        basis_h[strip, :] = high
        basis_l[strip, :] = low
    copies[1].wait()
    value = rhs[...]
    message[:rows, :] = dot3(value, basis_h[...], basis_l[...])
    message[rows : rows + 8, :] = to_rows([row_sum(value * value)], chosen.shape[1])
    copies[3].wait()
    copies[5].wait()
    params[...] = column_state([inverse, shift, jnp.broadcast_to(noise[...], (8, 1))])
    number = lax.axis_index("leaf") * anchors + lax.axis_index("sub")
    rank = keep.shape[1]
    slot = 0
    for base, bits in stages:
        for level in range(1, bits + 1):
            depth = base + level
            swap = (number >> (depth - 1)) & 1
            for p in range(1 << (bits - level)):
                heap = (1 << (total - depth)) - 1 + ((number >> depth) ^ p)
                row_chosen = keep[pl.ds(heap, 1), :]
                other = jnp.where(row_chosen < rank, row_chosen + rank, row_chosen - rank)
                chosen_out[slot : slot + 1, :] = jnp.where(swap == 1, other, row_chosen)
                slot += 1


def part_offsets(size, first, last):
    offsets = [0]
    for i in range(first, last):
        offsets.append(offsets[-1] + size - i * BLOCK)
    return offsets


def near_blocks(value, parts):
    rows, size = value.shape
    vh, vl = split(value)
    both = jnp.concatenate([vh, vl], axis=0)
    sums = [None] * (size // BLOCK)

    def three(cut, high, low, dims):
        wide = lax.dot_general(both[:, cut], high, dims, preferred_element_type=F32)
        thin = lax.dot_general(vh[:, cut], low, dims, preferred_element_type=F32)
        return wide[:rows] + wide[rows:] + thin

    def add(j, term):
        sums[j] = term if sums[j] is None else sums[j] + term

    for first, last, high, low in parts:
        offsets = part_offsets(size, first, last)
        for i in range(first, last):
            start, stop = offsets[i - first], offsets[i - first + 1]
            cut = slice(i * BLOCK, (i + 1) * BLOCK)
            out = three(cut, high[:, start:stop], low[:, start:stop], NN)
            for j in range(i, size // BLOCK):
                add(j, out[:, (j - i) * BLOCK : (j - i + 1) * BLOCK])
            if i + 1 < size // BLOCK:
                start += BLOCK
                add(i, three(slice((i + 1) * BLOCK, size), high[:, start:stop], low[:, start:stop], NT))
    zero = jnp.zeros((rows, BLOCK), F32)
    return jnp.concatenate([zero if s is None else s for s in sums], axis=1)


def dense_kernel(dims, first, last, more, *refs):
    pts_row, rhs = refs[:2]
    before, params = (refs[2], refs[3]) if more else (None, None)
    high, low, near, pts_col = refs[-4:]
    size = pts_row.shape[1]
    offsets = part_offsets(size, first, last)
    pts_col[...] = pts_row[...].T
    for i in range(first, last):
        start = offsets[i - first]

        def body(k, carry):
            strip = pl.ds(pl.multiple_of(k * STRIP, STRIP), STRIP)
            left = pts_col[pl.ds(pl.multiple_of(i * BLOCK + k * STRIP, STRIP), STRIP), :]
            for j in range(i, size // BLOCK):
                right = pts_row[:, j * BLOCK : (j + 1) * BLOCK]
                h, l = split(gauss(left, right, dims))
                part = slice(start + (j - i) * BLOCK, start + (j - i + 1) * BLOCK)
                high[strip, part] = h
                low[strip, part] = l
            return carry

        lax.fori_loop(0, BLOCK // STRIP, body, 0)
    value = rhs[...]
    out = near_blocks(value, [(first, last, high, low)])
    if more:
        out = out + before[...] + params[0:1, 2:3] * value
    near[...] = out


def levels_of(count):
    return count.bit_length() - 1


def tree_slots(count):
    slots = {}
    for level in range(1, levels_of(count) + 1):
        for p in range(count >> level):
            slots[level, p] = len(slots)
    return slots


def sweep_up(weights, transfer, couple, top):
    count = len(weights)
    slots = tree_slots(count)
    own_terms = []
    energy = None
    for level in range(1, levels_of(count) + 1):
        parents = []
        for p in range(count >> level):
            slot = slots[level, p]
            first, second = weights[2 * p], weights[2 * p + 1]
            crossed = dot3(second, couple[0][slot], couple[1][slot])
            term = row_sum(first * crossed)
            energy = term if energy is None else energy + term
            if p == 0:
                own_terms.append(crossed)
            if level < levels_of(count) or top:
                joined = jnp.concatenate([first, second], axis=1)
                parents.append(dot3(joined, transfer[0][slot], transfer[1][slot]))
        weights = parents
    return weights, own_terms, 2.0 * energy


def sweep_down(search, own_terms, transfer, count):
    slots = tree_slots(count)
    for level in range(levels_of(count), 0, -1):
        own = own_terms[level - 1]
        if search is not None:
            slot = slots[level, 0]
            half = own.shape[1]
            own = own + dot3(search, transfer[0][slot, :half], transfer[1][slot, :half], NT)
        search = own
    return search


def build_tree(dims, coords, chosen, params, transfer, couple, top):
    count = len(coords)
    slots = tree_slots(count)
    rank = coords[0].shape[1]
    inverse, shift = params[:, 0:1], params[:, 1:2]
    scaled = [(c - shift) * inverse for c in coords]
    for level in range(1, levels_of(count) + 1):
        parents, parents_scaled = [], []
        for p in range(count >> level):
            slot = slots[level, p]
            columns = scaled[2 * p].T, scaled[2 * p + 1].T
            for i in range(rank // STRIP):
                strip = slice(i * STRIP, (i + 1) * STRIP)
                high, low = split(gauss(columns[1][strip, :], scaled[2 * p], dims))
                couple[0][slot, strip, :] = high
                couple[1][slot, strip, :] = low
            if level == levels_of(count) and not top:
                continue
            joined = jnp.concatenate([coords[2 * p], coords[2 * p + 1]], axis=1)
            parent = pick(joined, chosen[slot : slot + 1, :])
            parent_scaled = (parent - shift) * inverse
            for side, column in enumerate(columns):
                for i in range(rank // STRIP):
                    strip = slice(i * STRIP, (i + 1) * STRIP)
                    target = slice(side * rank + i * STRIP, side * rank + (i + 1) * STRIP)
                    high, low = split(gauss(column[strip, :], parent_scaled, dims))
                    transfer[0][slot, target, :] = high
                    transfer[1][slot, target, :] = low
            parents.append(parent)
            parents_scaled.append(parent_scaled)
        coords, scaled = parents, parents_scaled
    return coords


def add_rows(messages, rows):
    total = messages[0][rows : rows + 8, :]
    for message in messages[1:]:
        total = total + message[rows : rows + 8, :]
    return total


def lower_first_kernel(dims, rows, count, offset, refs):
    messages = refs[:count]
    params, chosen = refs[count : count + 2]
    message, terms, transfer_h, transfer_l, couple_h, couple_l = refs[-6:]
    transfer, couple = (transfer_h, transfer_l), (couple_h, couple_l)
    coords = [m[rows + 8 :, :] for m in messages]
    picks = chosen[offset : offset + count - 1, :]
    coords = build_tree(dims, coords, picks, params, transfer, couple, True)
    lower_finish(rows, messages, message, terms, transfer, couple, True)
    message[rows + 8 :, :] = coords[0]


def lower_finish(rows, messages, message, terms, transfer, couple, top):
    weights, own_terms, energy = sweep_up([m[:rows, :] for m in messages], transfer, couple, top)
    for i, term in enumerate(own_terms):
        terms[i] = term
    dots = add_rows(messages, rows)
    message[:rows, :] = weights[0]
    extra = to_rows([jnp.zeros_like(energy)] * 7 + [energy], dots.shape[1])
    message[rows : rows + 8, :] = dots + extra


def lower_kernel(rows, count, top, refs):
    messages = refs[:count]
    transfer_h, transfer_l, couple_h, couple_l = refs[count : count + 4]
    message, terms = refs[count + 4 :]
    lower_finish(
        rows, messages, message, terms, (transfer_h, transfer_l), (couple_h, couple_l), top
    )


def upper_build(dims, rows, count, offset, refs):
    messages = refs[:count]
    params, chosen, transfer_h, transfer_l, couple_h, couple_l = refs[count:]
    coords = [m[rows + 8 :, :] for m in messages]
    picks = chosen[offset : offset + count - 1, :]
    build_tree(
        dims, coords, picks, params, (transfer_h, transfer_l), (couple_h, couple_l), False
    )


def far_field(rows, messages, upper, lower):
    count = len(messages)
    weights = [m[:rows, :] for m in messages]
    _, own_terms, energy = sweep_up(weights, upper[:2], upper[2:], False)
    search = sweep_down(None, own_terms, upper[:2], count)
    for terms, high, low in reversed(lower):
        depth = terms.shape[0]
        own_terms = [terms[i] for i in range(depth)]
        search = sweep_down(search, own_terms, (high, low), 1 << depth)
    sums = to_columns(add_rows(messages, rows), rows)
    return search, sums, sums[:, 7:8] + energy


def near_field(value, params, parts):
    return params[0:1, 2:3] * value + near_blocks(value, parts)


def column_state(columns):
    rows = columns[0].shape[0]
    lane = lax.broadcasted_iota(jnp.int32, (rows, 128), 1)
    block = jnp.zeros((rows, 128), F32)
    for i, column in enumerate(columns):
        block = jnp.where(lane == i, column, block)
    return block


def take_refs(refs, *sizes):
    groups = []
    position = 0
    for size in sizes:
        groups.append(refs[position : position + size])
        position += size
    groups.append(refs[position:])
    return groups


def open_refs(rows, count, stages, refs):
    messages, lower, upper, basis, rest = take_refs(refs, count, 3 * stages, 4, 2)
    lower = [lower[i : i + 3] for i in range(0, 3 * stages, 3)]
    return far_field(rows, messages, upper, lower), basis, rest


def dense_parts(cuts, refs):
    return [(*cut, refs[2 * i], refs[2 * i + 1]) for i, cut in enumerate(cuts)]


def first_kernel(rows, count, stages, cuts, refs):
    (search, sums, far), basis, rest = open_refs(rows, count, stages, refs)
    dense, rest = take_refs(rest, 2 * len(cuts))
    params, rhs, near_in, message, q_out, near_out, state = rest
    norm = sums[:, 0:1]
    rate = norm / (params[0:1, 2:3] * norm + jnp.abs(far))
    q = rate * (near_in[...] + dot3(search, basis[0][...], basis[1][...], NT))
    q_out[...] = q
    message[:rows, :] = dot3(q, basis[0][...], basis[1][...])
    near_q = near_field(q, params, dense_parts(cuts, dense))
    near_out[...] = near_q
    dots = [row_sum(rhs[...] * q), row_sum(q * q), row_sum(q * near_q)]
    message[rows:, :] = to_rows(dots, message.shape[1])
    state[...] = column_state([norm, rate])


def second_kernel(rows, count, stages, cuts, refs):
    (search, sums, far), basis, rest = open_refs(rows, count, stages, refs)
    dense, rest = take_refs(rest, 2 * len(cuts))
    params, rhs, q_in, near_in, state_in = rest[:5]
    message, x_out, r_out, d_out, q_out, near_out, state = rest[5:]
    norm0, rate = state_in[:, 0:1], state_in[:, 1:2]
    bq, qq, qaq = sums[:, 0:1], sums[:, 1:2], sums[:, 2:3] + far
    step = norm0 / bq
    alpha0 = step * rate
    norm1 = step * step * qq - norm0
    beta = norm1 / norm0
    back = 1.0 / rate
    rhs_v, q = rhs[...], q_in[...]
    r1 = rhs_v - step * q
    d1 = r1 + beta * rhs_v
    q0 = back * q
    aq = near_in[...] + dot3(search, basis[0][...], basis[1][...], NT)
    q1 = (1.0 + beta) * q0 - step * aq
    rar = back * (bq - 2.0 * step * qq) + step * step * qaq
    cross = back * (bq - step * qq)
    curve = rar + 2.0 * beta * cross + beta * beta * (back * bq)
    alpha1 = norm1 / curve
    x_out[...] = alpha0 * rhs_v + alpha1 * d1
    r2 = r1 - alpha1 * q1
    r_out[...] = r2
    d_out[...] = d1
    q_out[...] = q1
    message[:rows, :] = dot3(r2, basis[0][...], basis[1][...])
    near = near_field(r2, params, dense_parts(cuts, dense))
    near_out[...] = near
    dots = [row_sum(r2 * r2), row_sum(r2 * q1), row_sum(r2 * near)]
    message[rows:, :] = to_rows(dots, message.shape[1])
    state[...] = column_state([norm1, curve])


def last_kernel(rows, count, stages, refs):
    (search, sums, far), basis, rest = open_refs(rows, count, stages, refs)
    x_in, r_in, d_in, q_in, near_in, state_in, x_out, r_out = rest
    norm1, curve1 = state_in[:, 0:1], state_in[:, 1:2]
    norm2, cross, rar = sums[:, 0:1], sums[:, 1:2], sums[:, 2:3] + far
    beta = norm2 / norm1
    curve = rar + 2.0 * beta * cross + beta * beta * curve1
    alpha = norm2 / curve
    image = near_in[...] + dot3(search, basis[0][...], basis[1][...], NT) + beta * q_in[...]
    r2 = r_in[...]
    x_out[...] = x_in[...] + alpha * (r2 + beta * d_in[...])
    r_out[...] = r2 - alpha * image


def gather(value, stage):
    axis, shift, bits = stage
    size = lax.axis_size(axis)
    pairs = [[(i, i ^ (s << shift)) for i in range(size)] for s in range(1, 1 << bits)]
    return [value] + [lax.ppermute(value, axis, pair) for pair in pairs]


def refs_of(kernel, *args):
    return lambda *refs: kernel(*args, refs)


def body(points, targets, leaf_skel, node_keep, lengthscales, noise_var):
    dims, size = points.shape
    rows = targets.shape[0]
    rank = leaf_skel.shape[1]
    subs = lax.axis_size("sub")
    stages = []
    total = 0
    for axis in ("sub", "leaf"):
        axis_bits = levels_of(lax.axis_size(axis))
        for shift in range(0, axis_bits, 3):
            bits = min(3, axis_bits - shift)
            stages.append((total + shift, axis, shift, bits))
        total += axis_bits
    bases = tuple((base, bits) for base, _, _, bits in stages)
    hops = [stage[1:] for stage in stages]
    counts = [1 << bits for _, bits in bases]
    slots = sum(counts) - len(counts)
    offsets = [sum(counts[:i]) - i for i in range(len(counts))]
    stage_count = len(stages) - 1

    message, rhs, pts_row, basis_h, basis_l, chosen, params = call(
        functools.partial(setup_kernel, bases, total, subs),
        [
            f32_shape(rows + 16, rank),
            f32_shape(rows, size),
            f32_shape(8, size),
            bf16_shape(size, rank),
            bf16_shape(size, rank),
            jax.ShapeDtypeStruct((slots, rank), jnp.int32),
            f32_shape(8, 128),
        ],
        [
            points,
            targets,
            leaf_skel,
            node_keep,
            jnp.reshape(lengthscales, (1, dims)),
            jnp.reshape(noise_var, (1, 1)),
        ],
        anywhere=range(6),
        scratch=[
            pltpu.VMEM((dims, size), F32),
            pltpu.VMEM((1, rank), jnp.int32),
            pltpu.VMEM(node_keep.shape, jnp.int32),
            pltpu.VMEM((1, dims), F32),
            pltpu.VMEM((1, 1), F32),
            pltpu.VMEM((size, 8), F32),
            pltpu.SemaphoreType.DMA((6,)),
        ],
        name="setup",
    )
    basis = [basis_h, basis_l]

    def tree_shapes(count):
        nodes = count - 1
        return [bf16_shape(nodes, 2 * rank, rank)] * 2 + [bf16_shape(nodes, rank, rank)] * 2

    blocks = size // BLOCK
    cuts = [(0, blocks // 4), (blocks // 4, blocks)]
    dense = []

    def build_dense(cut, extra):
        width = part_offsets(size, *cut)[-1]
        high, low, near = call(
            functools.partial(dense_kernel, dims, *cut, len(extra) > 1),
            [bf16_shape(BLOCK, width), bf16_shape(BLOCK, width), f32_shape(rows, size)],
            [pts_row, rhs] + extra,
            scratch=[pltpu.VMEM((size, 8), F32)],
            cost=(12 * rows * BLOCK * width, BLOCK * width),
            name="dense",
        )
        dense.extend([high, low])
        return near

    trees = []
    terms_all = []
    near = None
    for i in range(stage_count):
        messages = gather(message, hops[i])
        extra = []
        if i == 0:
            near = build_dense(cuts[0], [])
            extra = [near]
        message, terms, *tree = call(
            refs_of(lower_first_kernel, dims, rows, counts[i], offsets[i]),
            [f32_shape(rows + 16, rank), f32_shape(bases[i][1], rows, rank)]
            + tree_shapes(counts[i]),
            messages + [params, chosen] + extra,
            name="lower_first",
        )
        trees.append(tree)
        terms_all.append(terms)
    messages = gather(message, hops[-1])
    near = build_dense(cuts[1], [near, params, message])
    upper = call(
        refs_of(upper_build, dims, rows, counts[-1], offsets[-1]),
        tree_shapes(counts[-1]),
        messages + [params, chosen],
        name="upper_build",
    )

    state_shape = f32_shape(rows, 128)
    vector = f32_shape(rows, size)
    message_shape = f32_shape(rows + 8, rank)

    def lower_of(terms_all):
        return [a for terms, tree in zip(terms_all, trees) for a in (terms, tree[0], tree[1])]

    def exchange(message):
        terms_all = []
        for i in range(stage_count):
            messages = gather(message, hops[i])
            message, terms = call(
                refs_of(lower_kernel, rows, counts[i], True),
                [message_shape, f32_shape(bases[i][1], rows, rank)],
                messages + trees[i],
                name="lower",
            )
            terms_all.append(terms)
        return gather(message, hops[-1]) + lower_of(terms_all)

    fixed = (rows, counts[-1], stage_count)
    message, q, near, state = call(
        refs_of(first_kernel, *fixed, cuts),
        [message_shape, vector, vector, state_shape],
        messages + lower_of(terms_all) + upper + basis + dense + [params, rhs, near],
        name="first",
    )
    arrived = exchange(message)
    message, x, r, d, q, near, state = call(
        refs_of(second_kernel, *fixed, cuts),
        [message_shape, vector, vector, vector, vector, vector, state_shape],
        arrived + upper + basis + dense + [params, rhs, q, near, state],
        name="second",
    )
    arrived = exchange(message)
    return tuple(
        call(
            refs_of(last_kernel, *fixed),
            [vector, vector],
            arrived + upper + basis + [x, r, d, q, near, state],
            name="last",
        )
    )


def solution(mesh):
    in_specs = (
        P(None, ("parts", "leaf", "sub")),
        P(None, ("parts", "leaf", "sub")),
        P(("parts", "leaf", "sub"), None),
        P("parts", None),
        P("parts"),
        P("parts"),
    )
    out_specs = (P(None, ("parts", "leaf", "sub")), P(None, ("parts", "leaf", "sub")))
    return jax.shard_map(body, mesh=mesh, in_specs=in_specs, out_specs=out_specs, check_vma=False)
```

```python
import functools
import math

import jax
import jax.numpy as jnp
from jax import lax
from jax.experimental import pallas as pl
from jax.experimental.pallas import tpu as pltpu
from jax.sharding import PartitionSpec as P

F32 = jnp.float32
BF16 = jnp.bfloat16
VMEM = pl.BlockSpec(memory_space=pltpu.VMEM)
ANY = pl.BlockSpec(memory_space=pl.ANY)
HBM = pltpu.MemorySpace.HBM
NN = (((1,), (0,)), ((), ()))
NT = (((1,), (1,)), ((), ()))
SCALE = math.sqrt(0.5 * math.log2(math.e))
STRIP = 256
BLOCK = 256


def resident_shape(*shape):
    return pltpu.VMEM(shape, BF16)


def is_resident(shape):
    return not isinstance(shape, jax.ShapeDtypeStruct)


def call(kernel, out_shape, args, anywhere=(), pinned=(), resident=(), scratch=(), name=None, cost=None):
    total = sum(a.size * a.dtype.itemsize for i, a in enumerate(args) if i not in anywhere)
    total += sum(math.prod(s.shape) * s.dtype.itemsize for s in out_shape)
    held = sum(a.size * a.dtype.itemsize for a in args if any(a is kept for kept in resident))
    held += sum(math.prod(s.shape) * s.dtype.itemsize for s in out_shape if is_resident(s))
    if cost is not None:
        cost = pl.CostEstimate(flops=cost[0], transcendentals=cost[1], bytes_accessed=total)
    args = [
        pltpu.with_memory_space_constraint(a, HBM) if i in pinned else a for i, a in enumerate(args)
    ]
    results = pl.pallas_call(
        kernel,
        out_shape=list(out_shape),
        in_specs=[ANY if i in anywhere else VMEM for i in range(len(args))],
        out_specs=[VMEM] * len(out_shape),
        scratch_shapes=list(scratch),
        compiler_params=pltpu.CompilerParams(vmem_limit_bytes=total - held + (6 << 20)),
        cost_estimate=cost,
        name=name,
    )(*args)
    return list(results)


def f32_shape(*shape):
    return jax.ShapeDtypeStruct(shape, F32)


def bf16_shape(*shape):
    return jax.ShapeDtypeStruct(shape, BF16)


def split(value):
    high = value.astype(BF16)
    return high, (value - high.astype(F32)).astype(BF16)


def split3(value):
    high = value.astype(BF16)
    rest = value - high.astype(F32)
    middle = rest.astype(BF16)
    return high, middle, (rest - middle.astype(F32)).astype(BF16)


def dot3(value, high, low, dims=NN):
    rows = value.shape[0]
    vh, vl = split(value)
    both = lax.dot_general(
        jnp.concatenate([vh, vl], axis=0), high, dims, preferred_element_type=F32
    )
    return both[:rows] + both[rows:] + lax.dot_general(vh, low, dims, preferred_element_type=F32)


def stack_scalars(first, second):
    row = lax.broadcasted_iota(jnp.int32, (8, first[0].shape[1]), 0)
    block = jnp.zeros(row.shape, F32)
    for i, value in enumerate(first + second):
        block = jnp.where(row == i, value, block)
    return block


def features(scaled, unit):
    value = scaled * (1.0 / unit)
    whole = jnp.floor(value + 0.5)
    part = value - whole
    f1, f2, f3 = (f.astype(F32) for f in split3(part))
    norm = jnp.sum(whole * whole, axis=0, keepdims=True)
    rest = jnp.sum(part * (2.0 * whole + part), axis=0, keepdims=True)
    norms = [-f.astype(F32) for f in split3(norm)]
    rests = [-f.astype(F32) for f in split3(rest)]
    ones = [jnp.ones_like(norm)] * 3
    twice = 2.0 * whole
    g1, g2, g3 = 2.0 * f1, 2.0 * f2, 2.0 * f3
    left = (
        jnp.concatenate([twice, stack_scalars(norms, ones)], axis=0),
        jnp.concatenate(
            [twice, twice, twice, g1, g2, g3, g1, g1, g2, stack_scalars(rests, ones)], axis=0
        ),
    )
    right = (
        jnp.concatenate([whole, stack_scalars(ones, norms)], axis=0),
        jnp.concatenate(
            [f1, f2, f3, whole, whole, whole, f1, f2, f1, stack_scalars(ones, rests)], axis=0
        ),
    )
    return tuple(a.T.astype(BF16) for a in left), tuple(a.astype(BF16) for a in right)


def unit_of(scaled):
    peak = jnp.max(jnp.max(jnp.abs(scaled), axis=1, keepdims=True), axis=0, keepdims=True)
    return jnp.maximum(peak, 1e-6) * (1.0 / 128.0)


def gauss(left, right, unit):
    squared = lax.dot_general(left[0], right[0], NN, preferred_element_type=F32)
    squared = squared + lax.dot_general(left[1], right[1], NN, preferred_element_type=F32)
    return jnp.exp2(squared * (unit * unit))


def pick(table, chosen):
    rows, pool = table.shape
    hit = lax.broadcasted_iota(jnp.int32, (pool, chosen.shape[1]), 0) == chosen
    onehot = jnp.where(hit, 1.0, 0.0).astype(BF16)
    parts = [lax.dot_general(t, onehot, NN, preferred_element_type=F32) for t in split3(table)]
    return parts[0] + parts[1] + parts[2]


def to_rows(columns, width):
    rows = columns[0].shape[0]
    lane = lax.broadcasted_iota(jnp.int32, (rows, 128), 1)
    block = jnp.zeros((rows, 128), F32)
    for i, column in enumerate(columns):
        block = jnp.where(lane == i, column, block)
    if rows < 128:
        block = jnp.concatenate([block, jnp.zeros((128 - rows, 128), F32)], axis=0)
    flipped = block.T[:8]
    return jnp.concatenate([flipped, jnp.zeros((8, width - 128), F32)], axis=1)


def to_columns(block, rows):
    square = jnp.concatenate([block[:, :128], jnp.zeros((120, 128), F32)], axis=0)
    return square.T[:rows]


def row_sum(value):
    return jnp.sum(value, axis=1, keepdims=True)


def setup_kernel(stages, total, anchors, *refs):
    sources, refs = refs[:6], refs[6:]
    message, rhs, la, lb, ra, rb, basis_h, basis_l, chosen_out, params = refs[:10]
    pts, skel, keep, scales, noise, sems = refs[10:]
    targets = (pts, rhs, skel, keep, scales, noise)
    copies = [
        pltpu.make_async_copy(source, target, sems.at[i])
        for i, (source, target) in enumerate(zip(sources, targets))
    ]
    for copy in copies:
        copy.start()
    for i in (0, 2, 4):
        copies[i].wait()
    dims, count = pts.shape
    points = jnp.concatenate([pts[...], jnp.zeros((8 - dims, count), F32)], axis=0)
    row = lax.broadcasted_iota(jnp.int32, (8, dims), 0)
    lane = lax.broadcasted_iota(jnp.int32, (8, dims), 1)
    spread = jnp.broadcast_to(scales[...], (8, dims))
    length = row_sum(jnp.where(row == lane, spread, 0.0))
    valid = lax.broadcasted_iota(jnp.int32, (8, 1), 0) < dims
    inverse = SCALE / jnp.where(valid, length, 1.0)
    low_end = jnp.min(points, axis=1, keepdims=True)
    shift = low_end + 0.5 * (jnp.max(points, axis=1, keepdims=True) - low_end)
    chosen = pick(points, skel[...])
    rows = rhs.shape[0]
    message[rows + 8 :, :] = chosen
    scaled = (points - shift) * inverse
    unit = unit_of(scaled)
    (la[...], lb[...]), (ra[...], rb[...]) = features(scaled, unit)
    _, own = features((chosen - shift) * inverse, unit)
    for i in range(count // STRIP):
        strip = slice(i * STRIP, (i + 1) * STRIP)
        high, low = split(gauss((la[strip, :], lb[strip, :]), own, unit))
        basis_h[strip, :] = high
        basis_l[strip, :] = low
    copies[1].wait()
    value = rhs[...]
    message[:rows, :] = dot3(value, basis_h[...], basis_l[...])
    message[rows : rows + 8, :] = to_rows([row_sum(value * value)], chosen.shape[1])
    copies[3].wait()
    copies[5].wait()
    params[...] = column_state(
        [inverse, shift, jnp.broadcast_to(noise[...], (8, 1)), jnp.broadcast_to(unit, (8, 1))]
    )
    number = lax.axis_index("leaf") * anchors + lax.axis_index("sub")
    rank = keep.shape[1]
    slot = 0
    for base, bits in stages:
        for level in range(1, bits + 1):
            depth = base + level
            swap = (number >> (depth - 1)) & 1
            for p in range(1 << (bits - level)):
                heap = (1 << (total - depth)) - 1 + ((number >> depth) ^ p)
                row_chosen = keep[pl.ds(heap, 1), :]
                other = jnp.where(row_chosen < rank, row_chosen + rank, row_chosen - rank)
                chosen_out[slot : slot + 1, :] = jnp.where(swap == 1, other, row_chosen)
                slot += 1


def near_blocks(value, parts):
    return jnp.concatenate([dot3(value, high[...], low[...]) for high, low in parts], axis=1)


def dense_kernel(start, la, lb, ra, rb, rhs, params, tie, high, low, near):
    size = la.shape[0]
    width = high.shape[1]
    unit = params[0:1, 3:4]

    def body(k, carry):
        strip = pl.ds(pl.multiple_of(k * STRIP, STRIP), STRIP)
        left = la[strip, :], lb[strip, :]
        for j in range(0, width, BLOCK):
            cut = slice(start + j, start + j + BLOCK)
            h, l = split(gauss(left, (ra[:, cut], rb[:, cut]), unit))
            high[strip, j : j + BLOCK] = h
            low[strip, j : j + BLOCK] = l
        return carry

    lax.fori_loop(0, size // STRIP, body, 0)
    value = rhs[...]
    here = value[:, start : start + width]
    near[...] = params[0:1, 2:3] * here + dot3(value, high[...], low[...])


def levels_of(count):
    return count.bit_length() - 1


def tree_slots(count):
    slots = {}
    for level in range(1, levels_of(count) + 1):
        for p in range(count >> level):
            slots[level, p] = len(slots)
    return slots


def sweep_up(weights, transfer, couple, top):
    count = len(weights)
    slots = tree_slots(count)
    own_terms = []
    energy = None
    for level in range(1, levels_of(count) + 1):
        parents = []
        for p in range(count >> level):
            slot = slots[level, p]
            first, second = weights[2 * p], weights[2 * p + 1]
            crossed = dot3(second, couple[0][slot], couple[1][slot])
            term = row_sum(first * crossed)
            energy = term if energy is None else energy + term
            if p == 0:
                own_terms.append(crossed)
            if level < levels_of(count) or top:
                joined = jnp.concatenate([first, second], axis=1)
                parents.append(dot3(joined, transfer[0][slot], transfer[1][slot]))
        weights = parents
    return weights, own_terms, 2.0 * energy


def sweep_down(search, own_terms, transfer, count):
    slots = tree_slots(count)
    for level in range(levels_of(count), 0, -1):
        own = own_terms[level - 1]
        if search is not None:
            slot = slots[level, 0]
            half = own.shape[1]
            own = own + dot3(search, transfer[0][slot, :half], transfer[1][slot, :half], NT)
        search = own
    return search


def build_tree(coords, chosen, params, transfer, couple, top):
    count = len(coords)
    slots = tree_slots(count)
    rank = coords[0].shape[1]
    inverse, shift = params[:, 0:1], params[:, 1:2]
    scaled = [(c - shift) * inverse for c in coords]
    unit = unit_of(jnp.concatenate(scaled, axis=1))
    sides = [features(c, unit) for c in scaled]
    for level in range(1, levels_of(count) + 1):
        parents, parent_sides = [], []
        for p in range(count >> level):
            slot = slots[level, p]
            high, low = split(gauss(sides[2 * p + 1][0], sides[2 * p][1], unit))
            couple[0][slot] = high
            couple[1][slot] = low
            if level == levels_of(count) and not top:
                continue
            joined = jnp.concatenate([coords[2 * p], coords[2 * p + 1]], axis=1)
            parent = pick(joined, chosen[slot : slot + 1, :])
            parent_side = features((parent - shift) * inverse, unit)
            for side in range(2):
                high, low = split(gauss(sides[2 * p + side][0], parent_side[1], unit))
                transfer[0][slot, side * rank : (side + 1) * rank, :] = high
                transfer[1][slot, side * rank : (side + 1) * rank, :] = low
            parents.append(parent)
            parent_sides.append(parent_side)
        coords, sides = parents, parent_sides
    return coords


def add_rows(messages, rows):
    total = messages[0][rows : rows + 8, :]
    for message in messages[1:]:
        total = total + message[rows : rows + 8, :]
    return total


def lower_first_kernel(rows, count, offset, refs):
    messages = refs[:count]
    params, chosen = refs[count : count + 2]
    message, terms, transfer_h, transfer_l, couple_h, couple_l = refs[-6:]
    transfer, couple = (transfer_h, transfer_l), (couple_h, couple_l)
    coords = [m[rows + 8 :, :] for m in messages]
    picks = chosen[offset : offset + count - 1, :]
    coords = build_tree(coords, picks, params, transfer, couple, True)
    lower_finish(rows, messages, message, terms, transfer, couple, True)
    message[rows + 8 :, :] = coords[0]


def lower_finish(rows, messages, message, terms, transfer, couple, top):
    weights, own_terms, energy = sweep_up([m[:rows, :] for m in messages], transfer, couple, top)
    for i, term in enumerate(own_terms):
        terms[i] = term
    dots = add_rows(messages, rows)
    message[:rows, :] = weights[0]
    extra = to_rows([jnp.zeros_like(energy)] * 7 + [energy], dots.shape[1])
    message[rows : rows + 8, :] = dots + extra


def lower_kernel(rows, count, top, refs):
    messages = refs[:count]
    transfer_h, transfer_l, couple_h, couple_l = refs[count : count + 4]
    message, terms = refs[count + 4 :]
    lower_finish(
        rows, messages, message, terms, (transfer_h, transfer_l), (couple_h, couple_l), top
    )


def upper_build(rows, count, offset, refs):
    messages = refs[:count]
    params, chosen, transfer_h, transfer_l, couple_h, couple_l = refs[count:]
    coords = [m[rows + 8 :, :] for m in messages]
    picks = chosen[offset : offset + count - 1, :]
    build_tree(
        coords, picks, params, (transfer_h, transfer_l), (couple_h, couple_l), False
    )


def far_field(rows, messages, upper, lower):
    count = len(messages)
    weights = [m[:rows, :] for m in messages]
    _, own_terms, energy = sweep_up(weights, upper[:2], upper[2:], False)
    search = sweep_down(None, own_terms, upper[:2], count)
    for terms, high, low in reversed(lower):
        depth = terms.shape[0]
        own_terms = [terms[i] for i in range(depth)]
        search = sweep_down(search, own_terms, (high, low), 1 << depth)
    sums = to_columns(add_rows(messages, rows), rows)
    return search, sums, sums[:, 7:8] + energy


def near_field(value, params, parts):
    return params[0:1, 2:3] * value + near_blocks(value, parts)


def column_state(columns):
    rows = columns[0].shape[0]
    lane = lax.broadcasted_iota(jnp.int32, (rows, 128), 1)
    block = jnp.zeros((rows, 128), F32)
    for i, column in enumerate(columns):
        block = jnp.where(lane == i, column, block)
    return block


def take_refs(refs, *sizes):
    groups = []
    position = 0
    for size in sizes:
        groups.append(refs[position : position + size])
        position += size
    groups.append(refs[position:])
    return groups


def open_refs(rows, count, stages, refs):
    messages, lower, upper, basis, rest = take_refs(refs, count, 3 * stages, 4, 2)
    lower = [lower[i : i + 3] for i in range(0, 3 * stages, 3)]
    return far_field(rows, messages, upper, lower), basis, rest


def dense_parts(refs):
    return list(zip(refs[0::2], refs[1::2]))


def first_kernel(rows, count, stages, parts, refs):
    (search, sums, far), basis, rest = open_refs(rows, count, stages, refs)
    dense, rest = take_refs(rest, 2 * parts)
    params, rhs = rest[:2]
    near_parts, (message, q_out, near_out, state) = take_refs(rest[2:], parts)
    near_b = jnp.concatenate([n[...] for n in near_parts], axis=1)
    norm = sums[:, 0:1]
    rate = norm / (params[0:1, 2:3] * norm + jnp.abs(far))
    q = rate * (near_b + dot3(search, basis[0][...], basis[1][...], NT))
    q_out[...] = q
    message[:rows, :] = dot3(q, basis[0][...], basis[1][...])
    near_q = near_field(q, params, dense_parts(dense))
    near_out[...] = near_q
    dots = [row_sum(rhs[...] * q), row_sum(q * q), row_sum(q * near_q)]
    message[rows:, :] = to_rows(dots, message.shape[1])
    state[...] = column_state([norm, rate])


def second_kernel(rows, count, stages, parts, refs):
    (search, sums, far), basis, rest = open_refs(rows, count, stages, refs)
    dense, rest = take_refs(rest, 2 * parts)
    params, rhs, q_in, near_in, state_in = rest[:5]
    message, x_out, r_out, d_out, q_out, near_out, state = rest[5:]
    norm0, rate = state_in[:, 0:1], state_in[:, 1:2]
    bq, qq, qaq = sums[:, 0:1], sums[:, 1:2], sums[:, 2:3] + far
    step = norm0 / bq
    alpha0 = step * rate
    norm1 = step * step * qq - norm0
    beta = norm1 / norm0
    back = 1.0 / rate
    rhs_v, q = rhs[...], q_in[...]
    r1 = rhs_v - step * q
    d1 = r1 + beta * rhs_v
    q0 = back * q
    aq = near_in[...] + dot3(search, basis[0][...], basis[1][...], NT)
    q1 = (1.0 + beta) * q0 - step * aq
    rar = back * (bq - 2.0 * step * qq) + step * step * qaq
    cross = back * (bq - step * qq)
    curve = rar + 2.0 * beta * cross + beta * beta * (back * bq)
    alpha1 = norm1 / curve
    x_out[...] = alpha0 * rhs_v + alpha1 * d1
    r2 = r1 - alpha1 * q1
    r_out[...] = r2
    d_out[...] = d1
    q_out[...] = q1
    message[:rows, :] = dot3(r2, basis[0][...], basis[1][...])
    near = near_field(r2, params, dense_parts(dense))
    near_out[...] = near
    dots = [row_sum(r2 * r2), row_sum(r2 * q1), row_sum(r2 * near)]
    message[rows:, :] = to_rows(dots, message.shape[1])
    state[...] = column_state([norm1, curve])


def last_kernel(rows, count, stages, refs):
    (search, sums, far), basis, rest = open_refs(rows, count, stages, refs)
    x_in, r_in, d_in, q_in, near_in, state_in, x_out, r_out = rest
    norm1, curve1 = state_in[:, 0:1], state_in[:, 1:2]
    norm2, cross, rar = sums[:, 0:1], sums[:, 1:2], sums[:, 2:3] + far
    beta = norm2 / norm1
    curve = rar + 2.0 * beta * cross + beta * beta * curve1
    alpha = norm2 / curve
    image = near_in[...] + dot3(search, basis[0][...], basis[1][...], NT) + beta * q_in[...]
    r2 = r_in[...]
    x_out[...] = x_in[...] + alpha * (r2 + beta * d_in[...])
    r_out[...] = r2 - alpha * image


def gather(value, stage):
    axis, shift, bits = stage
    size = lax.axis_size(axis)
    pairs = [[(i, i ^ (s << shift)) for i in range(size)] for s in range(1, 1 << bits)]
    return [value] + [lax.ppermute(value, axis, pair) for pair in pairs]


def refs_of(kernel, *args):
    return lambda *refs: kernel(*args, refs)


def body(points, targets, leaf_skel, node_keep, lengthscales, noise_var):
    dims, size = points.shape
    rows = targets.shape[0]
    rank = leaf_skel.shape[1]
    subs = lax.axis_size("sub")
    stages = []
    total = 0
    for axis in ("sub", "leaf"):
        axis_bits = levels_of(lax.axis_size(axis))
        for shift in range(0, axis_bits, 3):
            bits = min(3, axis_bits - shift)
            stages.append((total + shift, axis, shift, bits))
        total += axis_bits
    bases = tuple((base, bits) for base, _, _, bits in stages)
    hops = [stage[1:] for stage in stages]
    counts = [1 << bits for _, bits in bases]
    slots = sum(counts) - len(counts)
    offsets = [sum(counts[:i]) - i for i in range(len(counts))]
    stage_count = len(stages) - 1

    message, rhs, la, lb, ra, rb, basis_h, basis_l, chosen, params = call(
        functools.partial(setup_kernel, bases, total, subs),
        [
            f32_shape(rows + 16, rank),
            f32_shape(rows, size),
            bf16_shape(size, 16),
            bf16_shape(size, 80),
            bf16_shape(16, size),
            bf16_shape(80, size),
            bf16_shape(size, rank),
            bf16_shape(size, rank),
            jax.ShapeDtypeStruct((slots, rank), jnp.int32),
            f32_shape(8, 128),
        ],
        [
            points,
            targets,
            leaf_skel,
            node_keep,
            jnp.reshape(lengthscales, (1, dims)),
            jnp.reshape(noise_var, (1, 1)),
        ],
        anywhere=range(6),
        pinned=range(5),
        scratch=[
            pltpu.VMEM((dims, size), F32),
            pltpu.VMEM((1, rank), jnp.int32),
            pltpu.VMEM(node_keep.shape, jnp.int32),
            pltpu.VMEM((1, dims), F32),
            pltpu.VMEM((1, 1), F32),
            pltpu.SemaphoreType.DMA((6,)),
        ],
        name="setup",
    )
    basis = [basis_h, basis_l]

    def tree_shapes(count):
        nodes = count - 1
        return [bf16_shape(nodes, 2 * rank, rank)] * 2 + [bf16_shape(nodes, rank, rank)] * 2

    first_width = size // BLOCK * 3 // 8 * BLOCK
    widths = [first_width, size - first_width]
    dense, near_parts = [], []

    def build_dense(start, width, tie):
        high, low, near = call(
            functools.partial(dense_kernel, start),
            [resident_shape(size, width)] * 2 + [f32_shape(rows, width)],
            [la, lb, ra, rb, rhs, params, tie],
            cost=(6 * rows * size * width + 192 * size * width, size * width),
            name="dense",
        )
        dense.extend([high, low])
        near_parts.append(near)

    trees = []
    terms_all = []
    for i in range(stage_count):
        messages = gather(message, hops[i])
        extra = []
        if i == 0:
            build_dense(0, widths[0], params)
            extra = near_parts[:1]
        message, terms, *tree = call(
            refs_of(lower_first_kernel, rows, counts[i], offsets[i]),
            [f32_shape(rows + 16, rank), f32_shape(bases[i][1], rows, rank)]
            + tree_shapes(counts[i]),
            messages + [params, chosen] + extra,
            name="lower_first",
        )
        trees.append(tree)
        terms_all.append(terms)
    messages = gather(message, hops[-1])
    build_dense(widths[0], widths[1], message)
    upper = call(
        refs_of(upper_build, rows, counts[-1], offsets[-1]),
        tree_shapes(counts[-1]),
        messages + [params, chosen],
        name="upper_build",
    )

    state_shape = f32_shape(rows, 128)
    vector = f32_shape(rows, size)
    message_shape = f32_shape(rows + 8, rank)

    def lower_of(terms_all):
        return [a for terms, tree in zip(terms_all, trees) for a in (terms, tree[0], tree[1])]

    def exchange(message):
        terms_all = []
        for i in range(stage_count):
            messages = gather(message, hops[i])
            message, terms = call(
                refs_of(lower_kernel, rows, counts[i], True),
                [message_shape, f32_shape(bases[i][1], rows, rank)],
                messages + trees[i],
                name="lower",
            )
            terms_all.append(terms)
        return gather(message, hops[-1]) + lower_of(terms_all)

    fixed = (rows, counts[-1], stage_count)
    message, q, near, state = call(
        refs_of(first_kernel, *fixed, len(widths)),
        [message_shape, vector, vector, state_shape],
        messages + lower_of(terms_all) + upper + basis + dense + [params, rhs] + near_parts,
        resident=dense,
        name="first",
    )
    arrived = exchange(message)
    message, x, r, d, q, near, state = call(
        refs_of(second_kernel, *fixed, len(widths)),
        [message_shape, vector, vector, vector, vector, vector, state_shape],
        arrived + upper + basis + dense + [params, rhs, q, near, state],
        resident=dense,
        name="second",
    )
    arrived = exchange(message)
    return tuple(
        call(
            refs_of(last_kernel, *fixed),
            [vector, vector],
            arrived + upper + basis + [x, r, d, q, near, state],
            name="last",
        )
    )


def solution(mesh):
    in_specs = (
        P(None, ("parts", "leaf", "sub")),
        P(None, ("parts", "leaf", "sub")),
        P(("parts", "leaf", "sub"), None),
        P("parts", None),
        P("parts"),
        P("parts"),
    )
    out_specs = (P(None, ("parts", "leaf", "sub")), P(None, ("parts", "leaf", "sub")))
    return jax.shard_map(body, mesh=mesh, in_specs=in_specs, out_specs=out_specs, check_vma=False)
```

```python
import functools
import math

import jax
import jax.numpy as jnp
from jax import lax
from jax.experimental import pallas as pl
from jax.experimental.pallas import tpu as pltpu
from jax.sharding import PartitionSpec as P

F32 = jnp.float32
BF16 = jnp.bfloat16
VMEM = pl.BlockSpec(memory_space=pltpu.VMEM)
ANY = pl.BlockSpec(memory_space=pl.ANY)
HBM = pltpu.MemorySpace.HBM
NN = (((1,), (0,)), ((), ()))
NT = (((1,), (1,)), ((), ()))
SCALE = math.sqrt(0.5 * math.log2(math.e))
STRIP = 256
LANES = 128
BLOCK = 256


def resident_shape(*shape):
    return pltpu.VMEM(shape, BF16)


def is_resident(shape):
    return not isinstance(shape, jax.ShapeDtypeStruct)


def call(kernel, out_shape, args, anywhere=(), pinned=(), resident=(), copied=False, scratch=(), name=None, cost=None):
    total = sum(a.size * a.dtype.itemsize for i, a in enumerate(args) if i not in anywhere)
    total += sum(math.prod(s.shape) * s.dtype.itemsize for s in out_shape)
    held = sum(a.size * a.dtype.itemsize for a in args if any(a is kept for kept in resident))
    held += sum(math.prod(s.shape) * s.dtype.itemsize for s in out_shape if is_resident(s))
    if cost is not None:
        cost = pl.CostEstimate(flops=cost[0], transcendentals=cost[1], bytes_accessed=total)
    args = [
        pltpu.with_memory_space_constraint(a, HBM) if i in pinned else a for i, a in enumerate(args)
    ]
    results = pl.pallas_call(
        kernel,
        out_shape=list(out_shape),
        in_specs=[ANY if i in anywhere else VMEM for i in range(len(args))],
        out_specs=[ANY if copied else VMEM] * len(out_shape),
        scratch_shapes=list(scratch),
        compiler_params=pltpu.CompilerParams(vmem_limit_bytes=total - held + (6 << 20)),
        cost_estimate=cost,
        name=name,
    )(*args)
    return list(results)


def f32_shape(*shape):
    return jax.ShapeDtypeStruct(shape, F32)


def bf16_shape(*shape):
    return jax.ShapeDtypeStruct(shape, BF16)


def split(value):
    high = value.astype(BF16)
    return high, (value - high.astype(F32)).astype(BF16)


def split3(value):
    high = value.astype(BF16)
    rest = value - high.astype(F32)
    middle = rest.astype(BF16)
    return high, middle, (rest - middle.astype(F32)).astype(BF16)


def dot3(value, high, low, dims=NN):
    rows = value.shape[0]
    vh, vl = split(value)
    both = lax.dot_general(
        jnp.concatenate([vh, vl], axis=0), high, dims, preferred_element_type=F32
    )
    return both[:rows] + both[rows:] + lax.dot_general(vh, low, dims, preferred_element_type=F32)


def stack_scalars(first, second):
    row = lax.broadcasted_iota(jnp.int32, (8, first[0].shape[1]), 0)
    block = jnp.zeros(row.shape, F32)
    for i, value in enumerate(first + second):
        block = jnp.where(row == i, value, block)
    return block


def features(scaled, unit):
    value = scaled * (1.0 / unit)
    whole = jnp.floor(value + 0.5)
    part = value - whole
    f1, f2, f3 = (f.astype(F32) for f in split3(part))
    norm = jnp.sum(whole * whole, axis=0, keepdims=True)
    rest = jnp.sum(part * (2.0 * whole + part), axis=0, keepdims=True)
    norms = [-f.astype(F32) for f in split3(norm)]
    rests = [-f.astype(F32) for f in split3(rest)]
    ones = [jnp.ones_like(norm)] * 3
    twice = 2.0 * whole
    g1, g2, g3 = 2.0 * f1, 2.0 * f2, 2.0 * f3
    left = (
        jnp.concatenate([twice, stack_scalars(norms, ones)], axis=0),
        jnp.concatenate(
            [twice, twice, twice, g1, g2, g3, g1, g1, g2, stack_scalars(rests, ones)], axis=0
        ),
    )
    right = (
        jnp.concatenate([whole, stack_scalars(ones, norms)], axis=0),
        jnp.concatenate(
            [f1, f2, f3, whole, whole, whole, f1, f2, f1, stack_scalars(ones, rests)], axis=0
        ),
    )
    return tuple(a.T.astype(BF16) for a in left), tuple(a.astype(BF16) for a in right)


def unit_of(scaled):
    peak = jnp.max(jnp.max(jnp.abs(scaled), axis=1, keepdims=True), axis=0, keepdims=True)
    return jnp.maximum(peak, 1e-6) * (1.0 / 128.0)


def gauss(left, right, unit):
    squared = lax.dot_general(left[0], right[0], NN, preferred_element_type=F32)
    squared = squared + lax.dot_general(left[1], right[1], NN, preferred_element_type=F32)
    return jnp.exp2(squared * (unit * unit))


def pick(table, chosen):
    rows, pool = table.shape
    hit = lax.broadcasted_iota(jnp.int32, (pool, chosen.shape[1]), 0) == chosen
    onehot = jnp.where(hit, 1.0, 0.0).astype(BF16)
    stacked = jnp.concatenate([t.astype(F32) for t in split3(table)], axis=0).astype(BF16)
    parts = lax.dot_general(stacked, onehot, NN, preferred_element_type=F32)
    return parts[:rows] + parts[rows : 2 * rows] + parts[2 * rows :]


def write_wide(message, top, value):
    rows = value.shape[0]
    for k in range(value.shape[1] // LANES):
        start = top + k * rows
        message[start : start + rows, :] = value[:, k * LANES : (k + 1) * LANES]


def read_wide(message, top, rows, rank):
    starts = [top + k * rows for k in range(rank // LANES)]
    return jnp.concatenate([message[start : start + rows, :] for start in starts], axis=1)


def dots_at(rows, rank):
    return rows * (rank // LANES)


def message_rows(rows, rank, coords):
    return dots_at(rows, rank) + 8 + (dots_at(8, rank) if coords else 0)


def to_rows(columns):
    rows = columns[0].shape[0]
    block = column_state(columns)
    if rows < LANES:
        block = jnp.concatenate([block, jnp.zeros((LANES - rows, LANES), F32)], axis=0)
    return block.T[:8]


def to_columns(block, rows):
    square = jnp.concatenate([block, jnp.zeros((120, 128), F32)], axis=0)
    return square.T[:rows]


def row_sum(value):
    return jnp.sum(value, axis=1, keepdims=True)


def setup_kernel(stages, total, anchors, *refs):
    sources, refs = refs[:6], refs[6:]
    message, rhs, la, lb, ra, rb, basis_h, basis_l, chosen_out, params = refs[:10]
    pts, skel, keep, scales, noise, sems = refs[10:]
    targets = (pts, rhs, skel, keep, scales, noise)
    copies = [
        pltpu.make_async_copy(source, target, sems.at[i])
        for i, (source, target) in enumerate(zip(sources, targets))
    ]
    for copy in copies:
        copy.start()
    for i in (0, 2, 4):
        copies[i].wait()
    dims, count = pts.shape
    points = jnp.concatenate([pts[...], jnp.zeros((8 - dims, count), F32)], axis=0)
    row = lax.broadcasted_iota(jnp.int32, (8, dims), 0)
    lane = lax.broadcasted_iota(jnp.int32, (8, dims), 1)
    spread = jnp.broadcast_to(scales[...], (8, dims))
    length = row_sum(jnp.where(row == lane, spread, 0.0))
    valid = lax.broadcasted_iota(jnp.int32, (8, 1), 0) < dims
    inverse = SCALE / jnp.where(valid, length, 1.0)
    low_end = jnp.min(points, axis=1, keepdims=True)
    shift = low_end + 0.5 * (jnp.max(points, axis=1, keepdims=True) - low_end)
    chosen = pick(points, skel[...])
    rows = rhs.shape[0]
    rank = chosen.shape[1]
    dots = dots_at(rows, rank)
    write_wide(message, dots + 8, chosen)
    scaled = (points - shift) * inverse
    unit = unit_of(scaled)
    (la[...], lb[...]), (ra[...], rb[...]) = features(scaled, unit)
    _, own = features((chosen - shift) * inverse, unit)
    for i in range(count // STRIP):
        strip = slice(i * STRIP, (i + 1) * STRIP)
        high, low = split(gauss((la[strip, :], lb[strip, :]), own, unit))
        basis_h[strip, :] = high
        basis_l[strip, :] = low
    copies[1].wait()
    value = rhs[...]
    write_wide(message, 0, dot3(value, basis_h[...], basis_l[...]))
    message[dots : dots + 8, :] = to_rows([row_sum(value * value)])
    copies[3].wait()
    copies[5].wait()
    params[...] = column_state(
        [inverse, shift, jnp.broadcast_to(noise[...], (8, 1)), jnp.broadcast_to(unit, (8, 1))]
    )
    number = lax.axis_index("leaf") * anchors + lax.axis_index("sub")
    slot = 0
    for base, bits in stages:
        for level in range(1, bits + 1):
            depth = base + level
            swap = (number >> (depth - 1)) & 1
            for p in range(1 << (bits - level)):
                heap = (1 << (total - depth)) - 1 + ((number >> depth) ^ p)
                row_chosen = keep[pl.ds(heap, 1), :]
                other = jnp.where(row_chosen < rank, row_chosen + rank, row_chosen - rank)
                chosen_out[slot : slot + 1, :] = jnp.where(swap == 1, other, row_chosen)
                slot += 1


def near_blocks(value, parts):
    return jnp.concatenate([dot3(value, high[...], low[...]) for high, low in parts], axis=1)


def dense_kernel(start, la, lb, ra, rb, rhs, params, tie, high, low, near):
    size = la.shape[0]
    width = high.shape[1]
    unit = params[0:1, 3:4]

    def body(k, carry):
        strip = pl.ds(pl.multiple_of(k * STRIP, STRIP), STRIP)
        left = la[strip, :], lb[strip, :]
        for j in range(0, width, BLOCK):
            cut = slice(start + j, start + j + BLOCK)
            h, l = split(gauss(left, (ra[:, cut], rb[:, cut]), unit))
            high[strip, j : j + BLOCK] = h
            low[strip, j : j + BLOCK] = l
        return carry

    lax.fori_loop(0, size // STRIP, body, 0)
    value = rhs[...]
    here = value[:, start : start + width]
    near[...] = params[0:1, 2:3] * here + dot3(value, high[...], low[...])


def levels_of(count):
    return count.bit_length() - 1


def tree_slots(count):
    slots = {}
    for level in range(1, levels_of(count) + 1):
        for p in range(count >> level):
            slots[level, p] = len(slots)
    return slots


def sweep_up(weights, transfer, couple, top):
    count = len(weights)
    slots = tree_slots(count)
    own_terms = []
    energy = None
    for level in range(1, levels_of(count) + 1):
        parents = []
        for p in range(count >> level):
            slot = slots[level, p]
            first, second = weights[2 * p], weights[2 * p + 1]
            crossed = dot3(second, couple[0][slot], couple[1][slot])
            term = row_sum(first * crossed)
            energy = term if energy is None else energy + term
            if p == 0:
                own_terms.append(crossed)
            if level < levels_of(count) or top:
                joined = jnp.concatenate([first, second], axis=1)
                parents.append(dot3(joined, transfer[0][slot], transfer[1][slot]))
        weights = parents
    return weights, own_terms, 2.0 * energy


def sweep_down(search, own_terms, transfer, count):
    slots = tree_slots(count)
    for level in range(levels_of(count), 0, -1):
        own = own_terms[level - 1]
        if search is not None:
            slot = slots[level, 0]
            half = own.shape[1]
            own = own + dot3(search, transfer[0][slot, :half], transfer[1][slot, :half], NT)
        search = own
    return search


def build_tree(coords, chosen, params, transfer, couple, top):
    count = len(coords)
    slots = tree_slots(count)
    rank = coords[0].shape[1]
    inverse, shift = params[:, 0:1], params[:, 1:2]
    scaled = [(c - shift) * inverse for c in coords]
    unit = unit_of(jnp.concatenate(scaled, axis=1))
    sides = [features(c, unit) for c in scaled]
    for level in range(1, levels_of(count) + 1):
        parents, parent_sides = [], []
        for p in range(count >> level):
            slot = slots[level, p]
            high, low = split(gauss(sides[2 * p + 1][0], sides[2 * p][1], unit))
            couple[0][slot] = high
            couple[1][slot] = low
            if level == levels_of(count) and not top:
                continue
            joined = jnp.concatenate([coords[2 * p], coords[2 * p + 1]], axis=1)
            parent = pick(joined, chosen[slot : slot + 1, :])
            parent_side = features((parent - shift) * inverse, unit)
            for side in range(2):
                high, low = split(gauss(sides[2 * p + side][0], parent_side[1], unit))
                transfer[0][slot, side * rank : (side + 1) * rank, :] = high
                transfer[1][slot, side * rank : (side + 1) * rank, :] = low
            parents.append(parent)
            parent_sides.append(parent_side)
        coords, sides = parents, parent_sides
    return coords


def add_dots(messages, rows, rank):
    dots = slice(dots_at(rows, rank), dots_at(rows, rank) + 8)
    total = messages[0][dots, :]
    for message in messages[1:]:
        total = total + message[dots, :]
    return total


def coords_of(messages, rows, rank):
    return [read_wide(m, dots_at(rows, rank) + 8, 8, rank) for m in messages]


def weights_of(messages, rows, rank):
    return [read_wide(m, 0, rows, rank) for m in messages]


def lower_first_kernel(rows, count, offset, refs):
    messages = refs[:count]
    params, chosen = refs[count : count + 2]
    message, terms, transfer_h, transfer_l, couple_h, couple_l = refs[-6:]
    transfer, couple = (transfer_h, transfer_l), (couple_h, couple_l)
    rank = couple_h.shape[2]
    coords = coords_of(messages, rows, rank)
    picks = chosen[offset : offset + count - 1, :]
    coords = build_tree(coords, picks, params, transfer, couple, True)
    lower_finish(rows, messages, message, terms, transfer, couple, True)
    write_wide(message, dots_at(rows, rank) + 8, coords[0])


def lower_finish(rows, messages, message, terms, transfer, couple, top):
    rank = couple[0].shape[2]
    weights = weights_of(messages, rows, rank)
    weights, own_terms, energy = sweep_up(weights, transfer, couple, top)
    for i, term in enumerate(own_terms):
        terms[i] = term
    write_wide(message, 0, weights[0])
    dots = dots_at(rows, rank)
    extra = to_rows([jnp.zeros_like(energy)] * 7 + [energy])
    message[dots : dots + 8, :] = add_dots(messages, rows, rank) + extra


def lower_kernel(rows, count, top, refs):
    messages = refs[:count]
    transfer_h, transfer_l, couple_h, couple_l = refs[count : count + 4]
    message, terms = refs[count + 4 :]
    lower_finish(
        rows, messages, message, terms, (transfer_h, transfer_l), (couple_h, couple_l), top
    )


def upper_build(rows, count, offset, refs):
    messages = refs[:count]
    params, chosen, transfer_h, transfer_l, couple_h, couple_l = refs[count:]
    coords = coords_of(messages, rows, couple_h.shape[2])
    picks = chosen[offset : offset + count - 1, :]
    build_tree(
        coords, picks, params, (transfer_h, transfer_l), (couple_h, couple_l), False
    )


def own_chain(upper, lower):
    halves = []
    for high, low, count in lower + [upper]:
        slots = tree_slots(count)
        half = high.shape[2]
        for level in range(1, levels_of(count) + 1):
            slot = slots[level, 0]
            halves.append((high[slot, :half], low[slot, :half]))
    return halves[:-1]


def compose_kernel(counts, refs):
    high_out, low_out = refs[-2:]
    trees = [(refs[2 * i], refs[2 * i + 1], count) for i, count in enumerate(counts)]
    chain = own_chain(trees[-1], trees[:-1])
    rank = chain[0][0].shape[0]
    high, low = chain[0]
    for i in range(len(chain)):
        if i:
            product = high.astype(F32) + low.astype(F32)
            high, low = split(dot3(product, *chain[i]))
        high_out[:, i * rank : (i + 1) * rank] = high
        low_out[:, i * rank : (i + 1) * rank] = low


def far_field(rows, messages, upper, lower, path=None):
    count = len(messages)
    rank = upper[2].shape[2]
    weights = weights_of(messages, rows, rank)
    _, own_terms, energy = sweep_up(weights, upper[:2], upper[2:], False)
    sums = to_columns(add_dots(messages, rows, rank), rows)
    if path is None:
        search = sweep_down(None, own_terms, upper[:2], count)
        for terms, high, low in reversed(lower):
            depth = terms.shape[0]
            below = [terms[i] for i in range(depth)]
            search = sweep_down(search, below, (high, low), 1 << depth)
    else:
        below = [terms[i] for terms in lower for i in range(terms.shape[0])]
        search, *above = below + own_terms
        search = search + dot3(jnp.concatenate(above, axis=1), path[0][...], path[1][...], NT)
    return search, sums, sums[:, 7:8] + energy


def near_field(value, params, parts):
    return params[0:1, 2:3] * value + near_blocks(value, parts)


def column_state(columns):
    rows = columns[0].shape[0]
    lane = lax.broadcasted_iota(jnp.int32, (rows, 128), 1)
    block = jnp.zeros((rows, 128), F32)
    for i, column in enumerate(columns):
        block = jnp.where(lane == i, column, block)
    return block


def take_refs(refs, *sizes):
    groups = []
    position = 0
    for size in sizes:
        groups.append(refs[position : position + size])
        position += size
    groups.append(refs[position:])
    return groups


def open_refs(rows, count, stages, refs):
    messages, lower, upper, basis, rest = take_refs(refs, count, 3 * stages, 4, 2)
    lower = [lower[i : i + 3] for i in range(0, 3 * stages, 3)]
    return far_field(rows, messages, upper, lower), basis, rest


def open_composed(rows, count, stages, refs):
    messages, terms, upper, path, basis, rest = take_refs(refs, count, stages, 4, 2, 2)
    return far_field(rows, messages, upper, terms, path), basis, rest


def dense_parts(refs):
    return list(zip(refs[0::2], refs[1::2]))


def first_kernel(rows, count, stages, parts, refs):
    (search, sums, far), basis, rest = open_refs(rows, count, stages, refs)
    dense, rest = take_refs(rest, 2 * parts)
    params, rhs = rest[:2]
    near_parts, (message, q_out, near_out, state) = take_refs(rest[2:], parts)
    near_b = jnp.concatenate([n[...] for n in near_parts], axis=1)
    norm = sums[:, 0:1]
    rate = norm / (params[0:1, 2:3] * norm + jnp.abs(far))
    q = rate * (near_b + dot3(search, basis[0][...], basis[1][...], NT))
    q_out[...] = q
    write_wide(message, 0, dot3(q, basis[0][...], basis[1][...]))
    near_q = near_field(q, params, dense_parts(dense))
    near_out[...] = near_q
    dots = [row_sum(rhs[...] * q), row_sum(q * q), row_sum(q * near_q)]
    message[message.shape[0] - 8 :, :] = to_rows(dots)
    state[...] = column_state([norm, rate])


def second_kernel(rows, count, stages, parts, refs):
    (search, sums, far), basis, rest = open_composed(rows, count, stages, refs)
    dense, rest = take_refs(rest, 2 * parts)
    params, rhs, q_in, near_in, state_in = rest[:5]
    message, x_out, r_out, d_out, q_out, near_out, state = rest[5:]
    norm0, rate = state_in[:, 0:1], state_in[:, 1:2]
    bq, qq, qaq = sums[:, 0:1], sums[:, 1:2], sums[:, 2:3] + far
    step = norm0 / bq
    alpha0 = step * rate
    norm1 = step * step * qq - norm0
    beta = norm1 / norm0
    back = 1.0 / rate
    rhs_v, q = rhs[...], q_in[...]
    r1 = rhs_v - step * q
    d1 = r1 + beta * rhs_v
    q0 = back * q
    aq = near_in[...] + dot3(search, basis[0][...], basis[1][...], NT)
    q1 = (1.0 + beta) * q0 - step * aq
    rar = back * (bq - 2.0 * step * qq) + step * step * qaq
    cross = back * (bq - step * qq)
    curve = rar + 2.0 * beta * cross + beta * beta * (back * bq)
    alpha1 = norm1 / curve
    x_out[...] = alpha0 * rhs_v + alpha1 * d1
    r2 = r1 - alpha1 * q1
    r_out[...] = r2
    d_out[...] = d1
    q_out[...] = q1
    write_wide(message, 0, dot3(r2, basis[0][...], basis[1][...]))
    near = near_field(r2, params, dense_parts(dense))
    near_out[...] = near
    dots = [row_sum(r2 * r2), row_sum(r2 * q1), row_sum(r2 * near)]
    message[message.shape[0] - 8 :, :] = to_rows(dots)
    state[...] = column_state([norm1, curve])


def last_kernel(rows, count, stages, refs):
    (search, sums, far), basis, rest = open_composed(rows, count, stages, refs)
    x_in, r_in, d_in, q_in, near_in, state_in, x_out, r_out, x_done, r_done, sems = rest
    norm1, curve1 = state_in[:, 0:1], state_in[:, 1:2]
    norm2, cross, rar = sums[:, 0:1], sums[:, 1:2], sums[:, 2:3] + far
    beta = norm2 / norm1
    curve = rar + 2.0 * beta * cross + beta * beta * curve1
    alpha = norm2 / curve
    r2 = r_in[...]
    x_done[...] = x_in[...] + alpha * (r2 + beta * d_in[...])
    x_copy = pltpu.make_async_copy(x_done, x_out, sems.at[0])
    x_copy.start()
    image = near_in[...] + dot3(search, basis[0][...], basis[1][...], NT) + beta * q_in[...]
    r_done[...] = r2 - alpha * image
    r_copy = pltpu.make_async_copy(r_done, r_out, sems.at[1])
    r_copy.start()
    x_copy.wait()
    r_copy.wait()


def gather(value, stage):
    axis, shift, bits = stage
    size = lax.axis_size(axis)
    pairs = [[(i, i ^ (s << shift)) for i in range(size)] for s in range(1, 1 << bits)]
    return [value] + [lax.ppermute(value, axis, pair) for pair in pairs]


def refs_of(kernel, *args):
    return lambda *refs: kernel(*args, refs)


def body(points, targets, leaf_skel, node_keep, lengthscales, noise_var):
    dims, size = points.shape
    rows = targets.shape[0]
    rank = leaf_skel.shape[1]
    subs = lax.axis_size("sub")
    stages = []
    total = 0
    for axis in ("sub", "leaf"):
        axis_bits = levels_of(lax.axis_size(axis))
        for shift in range(0, axis_bits, 3):
            bits = min(3, axis_bits - shift)
            stages.append((total + shift, axis, shift, bits))
        total += axis_bits
    bases = tuple((base, bits) for base, _, _, bits in stages)
    hops = [stage[1:] for stage in stages]
    counts = [1 << bits for _, bits in bases]
    slots = sum(counts) - len(counts)
    offsets = [sum(counts[:i]) - i for i in range(len(counts))]
    stage_count = len(stages) - 1

    message, rhs, la, lb, ra, rb, basis_h, basis_l, chosen, params = call(
        functools.partial(setup_kernel, bases, total, subs),
        [
            f32_shape(message_rows(rows, rank, True), LANES),
            f32_shape(rows, size),
            bf16_shape(size, 16),
            bf16_shape(size, 80),
            bf16_shape(16, size),
            bf16_shape(80, size),
            bf16_shape(size, rank),
            bf16_shape(size, rank),
            jax.ShapeDtypeStruct((slots, rank), jnp.int32),
            f32_shape(8, 128),
        ],
        [
            points,
            targets,
            leaf_skel,
            node_keep,
            jnp.reshape(lengthscales, (1, dims)),
            jnp.reshape(noise_var, (1, 1)),
        ],
        anywhere=range(6),
        pinned=range(5),
        scratch=[
            pltpu.VMEM((dims, size), F32),
            pltpu.VMEM((1, rank), jnp.int32),
            pltpu.VMEM(node_keep.shape, jnp.int32),
            pltpu.VMEM((1, dims), F32),
            pltpu.VMEM((1, 1), F32),
            pltpu.SemaphoreType.DMA((6,)),
        ],
        name="setup",
    )
    basis = [basis_h, basis_l]

    def tree_shapes(count):
        nodes = count - 1
        return [bf16_shape(nodes, 2 * rank, rank)] * 2 + [bf16_shape(nodes, rank, rank)] * 2

    first_width = size // BLOCK * 3 // 8 * BLOCK
    widths = [first_width, size - first_width]
    dense, near_parts = [], []

    def build_dense(start, width, tie):
        high, low, near = call(
            functools.partial(dense_kernel, start),
            [resident_shape(size, width)] * 2 + [f32_shape(rows, width)],
            [la, lb, ra, rb, rhs, params, tie],
            cost=(6 * rows * size * width + 192 * size * width, size * width),
            name="dense",
        )
        dense.extend([high, low])
        near_parts.append(near)

    trees = []
    terms_all = []
    for i in range(stage_count):
        messages = gather(message, hops[i])
        extra = []
        if i == 0:
            build_dense(0, widths[0], params)
            extra = near_parts[:1]
        message, terms, *tree = call(
            refs_of(lower_first_kernel, rows, counts[i], offsets[i]),
            [f32_shape(message_rows(rows, rank, True), LANES), f32_shape(bases[i][1], rows, rank)]
            + tree_shapes(counts[i]),
            messages + [params, chosen] + extra,
            name="lower_first",
        )
        trees.append(tree)
        terms_all.append(terms)
    messages = gather(message, hops[-1])
    build_dense(widths[0], widths[1], message)
    upper = call(
        refs_of(upper_build, rows, counts[-1], offsets[-1]),
        tree_shapes(counts[-1]),
        messages + [params, chosen],
        name="upper_build",
    )

    state_shape = f32_shape(rows, 128)
    vector = f32_shape(rows, size)
    message_shape = f32_shape(message_rows(rows, rank, False), LANES)

    def lower_of(terms_all):
        return [a for terms, tree in zip(terms_all, trees) for a in (terms, tree[0], tree[1])]

    def exchange(message, shadow=None):
        terms_all = []
        made = None
        for i in range(stage_count):
            messages = gather(message, hops[i])
            if i == 0 and shadow is not None:
                made = shadow()
            message, terms = call(
                refs_of(lower_kernel, rows, counts[i], True),
                [message_shape, f32_shape(bases[i][1], rows, rank)],
                messages + trees[i],
                name="lower",
            )
            terms_all.append(terms)
        return gather(message, hops[-1]) + terms_all, made

    fixed = (rows, counts[-1], stage_count)
    message, q, near, state = call(
        refs_of(first_kernel, *fixed, len(widths)),
        [message_shape, vector, vector, state_shape],
        messages + lower_of(terms_all) + upper + basis + dense + [params, rhs] + near_parts,
        resident=dense,
        name="first",
    )

    def compose():
        pairs = [a for tree in trees + [upper] for a in tree[:2]]
        return call(
            refs_of(compose_kernel, counts),
            [bf16_shape(rank, (total - 1) * rank)] * 2,
            pairs + [state],
            cost=(12 * rank * rank * rank, 0),
            name="compose",
        )

    arrived, path = exchange(message, compose)
    message, x, r, d, q, near, state = call(
        refs_of(second_kernel, *fixed, len(widths)),
        [message_shape, vector, vector, vector, vector, vector, state_shape],
        arrived + upper + path + basis + dense + [params, rhs, q, near, state],
        resident=dense,
        name="second",
    )
    arrived, _ = exchange(message)
    return tuple(
        call(
            refs_of(last_kernel, *fixed),
            [vector, vector],
            arrived + upper + path + basis + [x, r, d, q, near, state],
            copied=True,
            scratch=[
                pltpu.VMEM((rows, size), F32),
                pltpu.VMEM((rows, size), F32),
                pltpu.SemaphoreType.DMA((2,)),
            ],
            name="last",
        )
    )


def solution(mesh):
    in_specs = (
        P(None, ("parts", "leaf", "sub")),
        P(None, ("parts", "leaf", "sub")),
        P(("parts", "leaf", "sub"), None),
        P("parts", None),
        P("parts"),
        P("parts"),
    )
    out_specs = (P(None, ("parts", "leaf", "sub")), P(None, ("parts", "leaf", "sub")))
    return jax.shard_map(body, mesh=mesh, in_specs=in_specs, out_specs=out_specs, check_vma=False)
```

```python
import functools
import math

import jax
import jax.numpy as jnp
from jax import lax
from jax.experimental import pallas as pl
from jax.experimental.pallas import tpu as pltpu
from jax.sharding import PartitionSpec as P

F32 = jnp.float32
BF16 = jnp.bfloat16
VMEM = pl.BlockSpec(memory_space=pltpu.VMEM)
ANY = pl.BlockSpec(memory_space=pl.ANY)
HBM = pltpu.MemorySpace.HBM
NN = (((1,), (0,)), ((), ()))
NT = (((1,), (1,)), ((), ()))
SCALE = math.sqrt(0.5 * math.log2(math.e))
STRIP = 256
LANES = 128
BLOCK = 256


def resident_shape(*shape):
    return pltpu.VMEM(shape, BF16)


def is_resident(shape):
    return not isinstance(shape, jax.ShapeDtypeStruct)


def call(kernel, out_shape, args, anywhere=(), pinned=(), resident=(), copied=False, scratch=(), name=None, cost=None):
    total = sum(a.size * a.dtype.itemsize for i, a in enumerate(args) if i not in anywhere)
    total += sum(math.prod(s.shape) * s.dtype.itemsize for s in out_shape)
    held = sum(a.size * a.dtype.itemsize for a in args if any(a is kept for kept in resident))
    held += sum(math.prod(s.shape) * s.dtype.itemsize for s in out_shape if is_resident(s))
    if cost is not None:
        cost = pl.CostEstimate(flops=cost[0], transcendentals=cost[1], bytes_accessed=total)
    args = [
        pltpu.with_memory_space_constraint(a, HBM) if i in pinned else a for i, a in enumerate(args)
    ]
    results = pl.pallas_call(
        kernel,
        out_shape=list(out_shape),
        in_specs=[ANY if i in anywhere else VMEM for i in range(len(args))],
        out_specs=[ANY if copied else VMEM] * len(out_shape),
        scratch_shapes=list(scratch),
        compiler_params=pltpu.CompilerParams(vmem_limit_bytes=total - held + (6 << 20)),
        cost_estimate=cost,
        name=name,
    )(*args)
    return list(results)


def f32_shape(*shape):
    return jax.ShapeDtypeStruct(shape, F32)


def bf16_shape(*shape):
    return jax.ShapeDtypeStruct(shape, BF16)


def split(value):
    high = value.astype(BF16)
    return high, (value - high.astype(F32)).astype(BF16)


def split3(value):
    high = value.astype(BF16)
    rest = value - high.astype(F32)
    middle = rest.astype(BF16)
    return high, middle, (rest - middle.astype(F32)).astype(BF16)


def doubled(value):
    both = jnp.concatenate(split(value), axis=0)
    return jnp.concatenate([both, both], axis=1)


def apply(wide, stacked, dims=NN):
    rows = wide.shape[0] // 2
    both = lax.dot_general(wide, stacked, dims, preferred_element_type=F32)
    return both[:rows] + both[rows:]


def product(value, stacked, dims=NN):
    return apply(doubled(value), stacked, dims)


def stack_scalars(first, second):
    row = lax.broadcasted_iota(jnp.int32, (8, first[0].shape[1]), 0)
    block = jnp.zeros(row.shape, F32)
    for i, value in enumerate(first + second):
        block = jnp.where(row == i, value, block)
    return block


def features(scaled, unit):
    value = scaled * (1.0 / unit)
    whole = jnp.floor(value + 0.5)
    part = value - whole
    f1, f2, f3 = (f.astype(F32) for f in split3(part))
    norm = jnp.sum(whole * whole, axis=0, keepdims=True)
    rest = jnp.sum(part * (2.0 * whole + part), axis=0, keepdims=True)
    norms = [-f.astype(F32) for f in split3(norm)]
    rests = [-f.astype(F32) for f in split3(rest)]
    ones = [jnp.ones_like(norm)] * 3
    twice = 2.0 * whole
    g1, g2, g3 = 2.0 * f1, 2.0 * f2, 2.0 * f3
    left = (
        jnp.concatenate([twice, stack_scalars(norms, ones)], axis=0),
        jnp.concatenate(
            [twice, twice, twice, g1, g2, g3, g1, g1, g2, stack_scalars(rests, ones)], axis=0
        ),
    )
    right = (
        jnp.concatenate([whole, stack_scalars(ones, norms)], axis=0),
        jnp.concatenate(
            [f1, f2, f3, whole, whole, whole, f1, f2, f1, stack_scalars(ones, rests)], axis=0
        ),
    )
    return tuple(a.T.astype(BF16) for a in left), tuple(a.astype(BF16) for a in right)


def unit_of(scaled):
    peak = jnp.max(jnp.max(jnp.abs(scaled), axis=1, keepdims=True), axis=0, keepdims=True)
    return jnp.maximum(peak, 1e-6) * (1.0 / 128.0)


def gauss(left, right, unit):
    squared = lax.dot_general(left[0], right[0], NN, preferred_element_type=F32)
    squared = squared + lax.dot_general(left[1], right[1], NN, preferred_element_type=F32)
    return jnp.exp2(squared * (unit * unit))


def pick(table, chosen):
    rows, pool = table.shape
    hit = lax.broadcasted_iota(jnp.int32, (pool, chosen.shape[1]), 0) == chosen
    onehot = jnp.where(hit, 1.0, 0.0).astype(BF16)
    stacked = jnp.concatenate([t.astype(F32) for t in split3(table)], axis=0).astype(BF16)
    parts = lax.dot_general(stacked, onehot, NN, preferred_element_type=F32)
    return parts[:rows] + parts[rows : 2 * rows] + parts[2 * rows :]


def write_wide(message, top, value):
    rows = value.shape[0]
    for k in range(value.shape[1] // LANES):
        start = top + k * rows
        message[start : start + rows, :] = value[:, k * LANES : (k + 1) * LANES]


def read_wide(message, top, rows, rank):
    starts = [top + k * rows for k in range(rank // LANES)]
    return jnp.concatenate([message[start : start + rows, :] for start in starts], axis=1)


def dots_at(rows, rank):
    return rows * (rank // LANES)


def message_rows(rows, rank, coords):
    return dots_at(rows, rank) + 8 + (dots_at(8, rank) if coords else 0)


def to_rows(columns):
    rows = columns[0].shape[0]
    block = column_state(columns)
    if rows < LANES:
        block = jnp.concatenate([block, jnp.zeros((LANES - rows, LANES), F32)], axis=0)
    return block.T[:8]


def to_columns(block, rows):
    square = jnp.concatenate([block, jnp.zeros((120, 128), F32)], axis=0)
    return square.T[:rows]


def row_sum(value):
    return jnp.sum(value, axis=1, keepdims=True)


def setup_kernel(stages, total, anchors, *refs):
    sources, refs = refs[:6], refs[6:]
    message, rhs, la, lb, ra, rb, basis, chosen_out, params = refs[:9]
    pts, skel, keep, scales, noise, sems = refs[9:]
    targets = (pts, rhs, skel, keep, scales, noise)
    copies = [
        pltpu.make_async_copy(source, target, sems.at[i])
        for i, (source, target) in enumerate(zip(sources, targets))
    ]
    for copy in copies:
        copy.start()
    for i in (0, 2, 4):
        copies[i].wait()
    dims, count = pts.shape
    points = jnp.concatenate([pts[...], jnp.zeros((8 - dims, count), F32)], axis=0)
    row = lax.broadcasted_iota(jnp.int32, (8, dims), 0)
    lane = lax.broadcasted_iota(jnp.int32, (8, dims), 1)
    spread = jnp.broadcast_to(scales[...], (8, dims))
    length = row_sum(jnp.where(row == lane, spread, 0.0))
    valid = lax.broadcasted_iota(jnp.int32, (8, 1), 0) < dims
    inverse = SCALE / jnp.where(valid, length, 1.0)
    low_end = jnp.min(points, axis=1, keepdims=True)
    shift = low_end + 0.5 * (jnp.max(points, axis=1, keepdims=True) - low_end)
    chosen = pick(points, skel[...])
    rows = rhs.shape[0]
    rank = chosen.shape[1]
    dots = dots_at(rows, rank)
    write_wide(message, dots + 8, chosen)
    scaled = (points - shift) * inverse
    unit = unit_of(scaled)
    (la[...], lb[...]), (ra[...], rb[...]) = features(scaled, unit)
    _, own = features((chosen - shift) * inverse, unit)
    for i in range(count // STRIP):
        strip = slice(i * STRIP, (i + 1) * STRIP)
        high, low = split(gauss((la[strip, :], lb[strip, :]), own, unit))
        basis[strip, :] = high
        basis[count + i * STRIP : count + (i + 1) * STRIP, :] = low
    copies[1].wait()
    value = rhs[...]
    write_wide(message, 0, product(value, basis[...]))
    message[dots : dots + 8, :] = to_rows([row_sum(value * value)])
    copies[3].wait()
    copies[5].wait()
    params[...] = column_state(
        [inverse, shift, jnp.broadcast_to(noise[...], (8, 1)), jnp.broadcast_to(unit, (8, 1))]
    )
    number = lax.axis_index("leaf") * anchors + lax.axis_index("sub")
    slot = 0
    for base, bits in stages:
        for level in range(1, bits + 1):
            depth = base + level
            swap = (number >> (depth - 1)) & 1
            for p in range(1 << (bits - level)):
                heap = (1 << (total - depth)) - 1 + ((number >> depth) ^ p)
                row_chosen = keep[pl.ds(heap, 1), :]
                other = jnp.where(row_chosen < rank, row_chosen + rank, row_chosen - rank)
                chosen_out[slot : slot + 1, :] = jnp.where(swap == 1, other, row_chosen)
                slot += 1


def dense_kernel(start, la, lb, ra, rb, rhs, params, tie, stacked, near):
    size, width = la.shape[0], stacked.shape[1]
    unit = params[0:1, 3:4]

    def body(k, carry):
        top = pl.multiple_of(k * STRIP, STRIP)
        strip, below = pl.ds(top, STRIP), pl.ds(pl.multiple_of(size + top, STRIP), STRIP)
        left = la[strip, :], lb[strip, :]
        for j in range(0, width, BLOCK):
            cut = slice(start + j, start + j + BLOCK)
            high, low = split(gauss(left, (ra[:, cut], rb[:, cut]), unit))
            stacked[strip, j : j + BLOCK] = high
            stacked[below, j : j + BLOCK] = low
        return carry

    lax.fori_loop(0, size // STRIP, body, 0, unroll=True)
    value = rhs[...]
    here = value[:, start : start + width]
    near[...] = params[0:1, 2:3] * here + product(value, stacked[...])


def flip_kernel(basis, tie, out):
    size, rank = basis.shape[0] // 2, basis.shape[1]
    for part in range(2):
        for i in range(0, size, STRIP):
            strip = basis[part * size + i : part * size + i + STRIP, :]
            out[part * rank : (part + 1) * rank, i : i + STRIP] = strip.T


def levels_of(count):
    return count.bit_length() - 1


def tree_slots(count):
    slots = {}
    for level in range(1, levels_of(count) + 1):
        for p in range(count >> level):
            slots[level, p] = len(slots)
    return slots


def sweep_up(weights, transfer, couple, top):
    count = len(weights)
    slots = tree_slots(count)
    own_terms = []
    energy = None
    for level in range(1, levels_of(count) + 1):
        parents = []
        for p in range(count >> level):
            slot = slots[level, p]
            first, second = weights[2 * p], weights[2 * p + 1]
            crossed = product(second, couple[slot])
            term = row_sum(first * crossed)
            energy = term if energy is None else energy + term
            if p == 0:
                own_terms.append(crossed)
            if level < levels_of(count) or top:
                joined = jnp.concatenate([first, second], axis=1)
                parents.append(product(joined, transfer[slot]))
        weights = parents
    return weights, own_terms, 2.0 * energy


def own_half(transfer, slot):
    rank = transfer.shape[2]
    return transfer[slot, :rank, :], transfer[slot, 2 * rank : 3 * rank, :]


def sweep_down(search, own_terms, transfer, count):
    slots = tree_slots(count)
    for level in range(levels_of(count), 0, -1):
        own = own_terms[level - 1]
        if search is not None:
            half = jnp.concatenate(own_half(transfer, slots[level, 0]), axis=1)
            own = own + product(search, half, NT)
        search = own
    return search


def build_tree(coords, chosen, params, transfer, couple, top):
    count = len(coords)
    slots = tree_slots(count)
    rank = coords[0].shape[1]
    inverse, shift = params[:, 0:1], params[:, 1:2]
    scaled = [(c - shift) * inverse for c in coords]
    unit = unit_of(jnp.concatenate(scaled, axis=1))
    sides = [features(c, unit) for c in scaled]
    for level in range(1, levels_of(count) + 1):
        parents, parent_sides = [], []
        for p in range(count >> level):
            slot = slots[level, p]
            high, low = split(gauss(sides[2 * p + 1][0], sides[2 * p][1], unit))
            couple[slot, :rank, :] = high
            couple[slot, rank:, :] = low
            if level == levels_of(count) and not top:
                continue
            joined = jnp.concatenate([coords[2 * p], coords[2 * p + 1]], axis=1)
            parent = pick(joined, chosen[slot : slot + 1, :])
            parent_side = features((parent - shift) * inverse, unit)
            for side in range(2):
                high, low = split(gauss(sides[2 * p + side][0], parent_side[1], unit))
                transfer[slot, side * rank : (side + 1) * rank, :] = high
                transfer[slot, (side + 2) * rank : (side + 3) * rank, :] = low
            parents.append(parent)
            parent_sides.append(parent_side)
        coords, sides = parents, parent_sides
    return coords


def add_dots(messages, rows, rank):
    dots = slice(dots_at(rows, rank), dots_at(rows, rank) + 8)
    total = messages[0][dots, :]
    for message in messages[1:]:
        total = total + message[dots, :]
    return total


def coords_of(messages, rows, rank):
    return [read_wide(m, dots_at(rows, rank) + 8, 8, rank) for m in messages]


def weights_of(messages, rows, rank):
    return [read_wide(m, 0, rows, rank) for m in messages]


def lower_first_kernel(rows, count, offset, refs):
    messages = refs[:count]
    params, chosen = refs[count : count + 2]
    message, terms, transfer, couple = refs[-4:]
    rank = couple.shape[2]
    coords = coords_of(messages, rows, rank)
    picks = chosen[offset : offset + count - 1, :]
    coords = build_tree(coords, picks, params, transfer, couple, True)
    lower_finish(rows, messages, message, terms, transfer, couple, True)
    write_wide(message, dots_at(rows, rank) + 8, coords[0])


def lower_finish(rows, messages, message, terms, transfer, couple, top):
    rank = couple.shape[2]
    weights = weights_of(messages, rows, rank)
    weights, own_terms, energy = sweep_up(weights, transfer, couple, top)
    for i, term in enumerate(own_terms):
        terms[i] = term
    write_wide(message, 0, weights[0])
    dots = dots_at(rows, rank)
    extra = to_rows([jnp.zeros_like(energy)] * 7 + [energy])
    message[dots : dots + 8, :] = add_dots(messages, rows, rank) + extra


def lower_kernel(rows, count, top, refs):
    transfer, couple, message, terms = refs[count:]
    lower_finish(rows, refs[:count], message, terms, transfer, couple, top)


def upper_build(rows, count, offset, refs):
    params, chosen, transfer, couple = refs[count:]
    coords = coords_of(refs[:count], rows, couple.shape[2])
    picks = chosen[offset : offset + count - 1, :]
    build_tree(coords, picks, params, transfer, couple, False)


def compose_kernel(counts, refs):
    out = refs[-1]
    halves = []
    for transfer, count in zip(refs, counts):
        slots = tree_slots(count)
        halves += [own_half(transfer, slots[i, 0]) for i in range(1, levels_of(count) + 1)]
    halves = halves[:-1]
    rank = out.shape[1]
    high, low = halves[0]
    for i, half in enumerate(halves):
        if i:
            chained = high.astype(F32) + low.astype(F32)
            high, low = split(product(chained, jnp.concatenate(half, axis=0)))
        out[i * rank : (i + 1) * rank, :] = high.T
        out[(len(halves) + i) * rank : (len(halves) + i + 1) * rank, :] = low.T


def far_field(rows, messages, upper, lower, path=None):
    count = len(messages)
    transfer, couple = upper
    rank = couple.shape[2]
    weights = weights_of(messages, rows, rank)
    _, own_terms, energy = sweep_up(weights, transfer, couple, False)
    sums = to_columns(add_dots(messages, rows, rank), rows)
    if path is None:
        search = sweep_down(None, own_terms, transfer, count)
        for terms, below_transfer in reversed(lower):
            depth = terms.shape[0]
            below = [terms[i] for i in range(depth)]
            search = sweep_down(search, below, below_transfer, 1 << depth)
    else:
        below = [terms[i] for terms in lower for i in range(terms.shape[0])]
        search, *above = below + own_terms
        search = search + product(jnp.concatenate(above, axis=1), path[...])
    return search, sums, sums[:, 7:8] + energy


def near_field(wide, value, params, parts):
    cuts = [apply(wide, part[...]) for part in parts]
    return params[0:1, 2:3] * value + jnp.concatenate(cuts, axis=1)


def column_state(columns):
    rows = columns[0].shape[0]
    lane = lax.broadcasted_iota(jnp.int32, (rows, 128), 1)
    block = jnp.zeros((rows, 128), F32)
    for i, column in enumerate(columns):
        block = jnp.where(lane == i, column, block)
    return block


def take_refs(refs, *sizes):
    groups = []
    position = 0
    for size in sizes:
        groups.append(refs[position : position + size])
        position += size
    groups.append(refs[position:])
    return groups


def open_refs(rows, count, stages, refs):
    messages, lower, upper, basis, rest = take_refs(refs, count, 2 * stages, 2, 2)
    lower = [lower[i : i + 2] for i in range(0, 2 * stages, 2)]
    return far_field(rows, messages, upper, lower), basis, rest


def open_composed(rows, count, stages, refs):
    messages, terms, upper, path, basis, rest = take_refs(refs, count, stages, 2, 1, 2)
    return far_field(rows, messages, upper, terms, path[0]), basis, rest


def first_kernel(rows, count, stages, parts, refs):
    (search, sums, far), basis, rest = open_refs(rows, count, stages, refs)
    dense, rest = take_refs(rest, parts)
    params, rhs = rest[:2]
    near_parts, (message, q_out, near_out, state) = take_refs(rest[2:], parts)
    near_b = jnp.concatenate([n[...] for n in near_parts], axis=1)
    norm = sums[:, 0:1]
    rate = norm / (params[0:1, 2:3] * norm + jnp.abs(far))
    q = rate * (near_b + product(search, basis[1][...]))
    q_out[...] = q
    wide = doubled(q)
    write_wide(message, 0, apply(wide, basis[0][...]))
    near_q = near_field(wide, q, params, dense)
    near_out[...] = near_q
    dots = [row_sum(rhs[...] * q), row_sum(q * q), row_sum(q * near_q)]
    message[message.shape[0] - 8 :, :] = to_rows(dots)
    state[...] = column_state([norm, rate])


def second_kernel(rows, count, stages, parts, refs):
    (search, sums, far), basis, rest = open_composed(rows, count, stages, refs)
    dense, rest = take_refs(rest, parts)
    params, rhs, q_in, near_in, state_in = rest[:5]
    message, r_out, q_out, near_out, state = rest[5:]
    norm0, rate = state_in[:, 0:1], state_in[:, 1:2]
    bq, qq, qaq = sums[:, 0:1], sums[:, 1:2], sums[:, 2:3] + far
    step = norm0 / bq
    alpha0 = step * rate
    norm1 = step * step * qq - norm0
    beta = norm1 / norm0
    back = 1.0 / rate
    rhs_v, q = rhs[...], q_in[...]
    r1 = rhs_v - step * q
    q0 = back * q
    aq = near_in[...] + product(search, basis[1][...])
    q1 = (1.0 + beta) * q0 - step * aq
    rar = back * (bq - 2.0 * step * qq) + step * step * qaq
    cross = back * (bq - step * qq)
    curve = rar + 2.0 * beta * cross + beta * beta * (back * bq)
    alpha1 = norm1 / curve
    r2 = r1 - alpha1 * q1
    r_out[...] = r2
    q_out[...] = q1
    wide = doubled(r2)
    write_wide(message, 0, apply(wide, basis[0][...]))
    near = near_field(wide, r2, params, dense)
    near_out[...] = near
    dots = [row_sum(r2 * r2), row_sum(r2 * q1), row_sum(r2 * near)]
    message[message.shape[0] - 8 :, :] = to_rows(dots)
    state[...] = column_state([norm1, curve, alpha0, alpha1, step, beta])


def update_kernel(rhs, q, state, x_out, d_out):
    alpha0, alpha1, step, beta = (state[:, i : i + 1] for i in range(2, 6))
    rhs_v = rhs[...]
    d1 = rhs_v - step * q[...] + beta * rhs_v
    d_out[...] = d1
    x_out[...] = alpha0 * rhs_v + alpha1 * d1


def last_kernel(rows, count, stages, refs):
    (search, sums, far), basis, rest = open_composed(rows, count, stages, refs)
    x_in, r_in, d_in, q_in, near_in, state_in, x_out, r_out, x_done, r_done, sems = rest
    norm1, curve1 = state_in[:, 0:1], state_in[:, 1:2]
    norm2, cross, rar = sums[:, 0:1], sums[:, 1:2], sums[:, 2:3] + far
    beta = norm2 / norm1
    curve = rar + 2.0 * beta * cross + beta * beta * curve1
    alpha = norm2 / curve
    r2 = r_in[...]
    x_done[...] = x_in[...] + alpha * (r2 + beta * d_in[...])
    x_copy = pltpu.make_async_copy(x_done, x_out, sems.at[0])
    x_copy.start()
    image = near_in[...] + product(search, basis[1][...]) + beta * q_in[...]
    r_done[...] = r2 - alpha * image
    r_copy = pltpu.make_async_copy(r_done, r_out, sems.at[1])
    r_copy.start()
    x_copy.wait()
    r_copy.wait()


def gather(value, stage):
    axis, shift, bits = stage
    size = lax.axis_size(axis)
    pairs = [[(i, i ^ (s << shift)) for i in range(size)] for s in range(1, 1 << bits)]
    return [value] + [lax.ppermute(value, axis, pair) for pair in pairs]


def refs_of(kernel, *args):
    return lambda *refs: kernel(*args, refs)


def body(points, targets, leaf_skel, node_keep, lengthscales, noise_var):
    dims, size = points.shape
    rows = targets.shape[0]
    rank = leaf_skel.shape[1]
    subs = lax.axis_size("sub")
    stages = []
    total = 0
    for axis in ("sub", "leaf"):
        axis_bits = levels_of(lax.axis_size(axis))
        for shift in range(0, axis_bits, 3):
            bits = min(3, axis_bits - shift)
            stages.append((total + shift, axis, shift, bits))
        total += axis_bits
    bases = tuple((base, bits) for base, _, _, bits in stages)
    hops = [stage[1:] for stage in stages]
    counts = [1 << bits for _, bits in bases]
    slots = sum(counts) - len(counts)
    offsets = [sum(counts[:i]) - i for i in range(len(counts))]
    stage_count = len(stages) - 1

    message, rhs, la, lb, ra, rb, basis, chosen, params = call(
        functools.partial(setup_kernel, bases, total, subs),
        [
            f32_shape(message_rows(rows, rank, True), LANES),
            f32_shape(rows, size),
            bf16_shape(size, 16),
            bf16_shape(size, 80),
            bf16_shape(16, size),
            bf16_shape(80, size),
            bf16_shape(2 * size, rank),
            jax.ShapeDtypeStruct((slots, rank), jnp.int32),
            f32_shape(8, 128),
        ],
        [
            points,
            targets,
            leaf_skel,
            node_keep,
            jnp.reshape(lengthscales, (1, dims)),
            jnp.reshape(noise_var, (1, 1)),
        ],
        anywhere=range(6),
        pinned=range(5),
        scratch=[
            pltpu.VMEM((dims, size), F32),
            pltpu.VMEM((1, rank), jnp.int32),
            pltpu.VMEM(node_keep.shape, jnp.int32),
            pltpu.VMEM((1, dims), F32),
            pltpu.VMEM((1, 1), F32),
            pltpu.SemaphoreType.DMA((6,)),
        ],
        name="setup",
    )

    def tree_shapes(count):
        nodes = count - 1
        return [bf16_shape(nodes, 4 * rank, rank), bf16_shape(nodes, 2 * rank, rank)]

    first_width = size // BLOCK * 3 // 8 * BLOCK
    widths = [first_width, size - first_width]
    dense, near_parts = [], []

    def build_dense(start, width, tie):
        stacked, near = call(
            functools.partial(dense_kernel, start),
            [resident_shape(2 * size, width), f32_shape(rows, width)],
            [la, lb, ra, rb, rhs, params, tie],
            cost=(6 * rows * size * width + 192 * size * width, size * width),
            name="dense",
        )
        dense.append(stacked)
        near_parts.append(near)

    trees = []
    terms_all = []
    for i in range(stage_count):
        messages = gather(message, hops[i])
        extra = []
        if i == 0:
            build_dense(0, widths[0], params)
            extra = near_parts[:1]
        message, terms, *tree = call(
            refs_of(lower_first_kernel, rows, counts[i], offsets[i]),
            [f32_shape(message_rows(rows, rank, True), LANES), f32_shape(bases[i][1], rows, rank)]
            + tree_shapes(counts[i]),
            messages + [params, chosen] + extra,
            name="lower_first",
        )
        trees.append(tree)
        terms_all.append(terms)
    messages = gather(message, hops[-1])
    build_dense(widths[0], widths[1], message)
    (flipped,) = call(
        flip_kernel,
        [bf16_shape(2 * rank, size)],
        [basis, message],
        cost=(64 * size * rank, 0),
        name="flip",
    )
    basis = [basis, flipped]
    upper = call(
        refs_of(upper_build, rows, counts[-1], offsets[-1]),
        tree_shapes(counts[-1]),
        messages + [params, chosen],
        name="upper_build",
    )

    state_shape = f32_shape(rows, 128)
    vector = f32_shape(rows, size)
    message_shape = f32_shape(message_rows(rows, rank, False), LANES)

    def lower_of(terms_all):
        return [a for terms, tree in zip(terms_all, trees) for a in (terms, tree[0])]

    def exchange(message, shadow=None):
        terms_all = []
        made = None
        for i in range(stage_count):
            messages = gather(message, hops[i])
            if i == 0 and shadow is not None:
                made = shadow()
            message, terms = call(
                refs_of(lower_kernel, rows, counts[i], True),
                [message_shape, f32_shape(bases[i][1], rows, rank)],
                messages + trees[i],
                name="lower",
            )
            terms_all.append(terms)
        return gather(message, hops[-1]) + terms_all, made

    fixed = (rows, counts[-1], stage_count)
    message, q, near, state = call(
        refs_of(first_kernel, *fixed, len(widths)),
        [message_shape, vector, vector, state_shape],
        messages + lower_of(terms_all) + upper + basis + dense + [params, rhs] + near_parts,
        resident=dense,
        name="first",
    )

    def compose():
        pairs = [tree[0] for tree in trees + [upper]]
        return call(
            refs_of(compose_kernel, counts),
            [bf16_shape(2 * (total - 1) * rank, rank)],
            pairs + [state],
            cost=(12 * rank * rank * rank, 0),
            name="compose",
        )

    arrived, path = exchange(message, compose)
    first_q = q
    message, r, q, near, state = call(
        refs_of(second_kernel, *fixed, len(widths)),
        [message_shape, vector, vector, vector, state_shape],
        arrived + upper + path + basis + dense + [params, rhs, q, near, state],
        resident=dense,
        name="second",
    )

    def update():
        return call(
            update_kernel,
            [vector, vector],
            [rhs, first_q, state],
            cost=(8 * rows * size, 0),
            name="update",
        )

    arrived, (x, d) = exchange(message, update)
    return tuple(
        call(
            refs_of(last_kernel, *fixed),
            [vector, vector],
            arrived + upper + path + basis + [x, r, d, q, near, state],
            copied=True,
            scratch=[
                pltpu.VMEM((rows, size), F32),
                pltpu.VMEM((rows, size), F32),
                pltpu.SemaphoreType.DMA((2,)),
            ],
            name="last",
        )
    )


def solution(mesh):
    in_specs = (
        P(None, ("parts", "leaf", "sub")),
        P(None, ("parts", "leaf", "sub")),
        P(("parts", "leaf", "sub"), None),
        P("parts", None),
        P("parts"),
        P("parts"),
    )
    out_specs = (P(None, ("parts", "leaf", "sub")), P(None, ("parts", "leaf", "sub")))
    return jax.shard_map(body, mesh=mesh, in_specs=in_specs, out_specs=out_specs, check_vma=False)
```

```python
import functools
import math

import jax
import jax.numpy as jnp
from jax import lax
from jax.experimental import pallas as pl
from jax.experimental.pallas import tpu as pltpu
from jax.sharding import PartitionSpec as P

F32 = jnp.float32
BF16 = jnp.bfloat16
VMEM = pl.BlockSpec(memory_space=pltpu.VMEM)
ANY = pl.BlockSpec(memory_space=pl.ANY)
HBM = pltpu.MemorySpace.HBM
NN = (((1,), (0,)), ((), ()))
NT = (((1,), (1,)), ((), ()))
SCALE = math.sqrt(0.5 * math.log2(math.e))
STRIP = 256
LANES = 128
BLOCK = 256


def resident_shape(*shape):
    return pltpu.VMEM(shape, BF16)


def is_resident(shape):
    return not isinstance(shape, jax.ShapeDtypeStruct)


def call(kernel, out_shape, args, anywhere=(), pinned=(), resident=(), copied=False, scratch=(), name=None, cost=None):
    total = sum(a.size * a.dtype.itemsize for i, a in enumerate(args) if i not in anywhere)
    total += sum(math.prod(s.shape) * s.dtype.itemsize for s in out_shape)
    held = sum(a.size * a.dtype.itemsize for a in args if any(a is kept for kept in resident))
    held += sum(math.prod(s.shape) * s.dtype.itemsize for s in out_shape if is_resident(s))
    if cost is not None:
        cost = pl.CostEstimate(flops=cost[0], transcendentals=cost[1], bytes_accessed=total)
    args = [
        pltpu.with_memory_space_constraint(a, HBM) if i in pinned else a for i, a in enumerate(args)
    ]
    results = pl.pallas_call(
        kernel,
        out_shape=list(out_shape),
        in_specs=[ANY if i in anywhere else VMEM for i in range(len(args))],
        out_specs=[ANY if copied else VMEM] * len(out_shape),
        scratch_shapes=list(scratch),
        compiler_params=pltpu.CompilerParams(vmem_limit_bytes=total - held + (6 << 20)),
        cost_estimate=cost,
        name=name,
    )(*args)
    return list(results)


def f32_shape(*shape):
    return jax.ShapeDtypeStruct(shape, F32)


def bf16_shape(*shape):
    return jax.ShapeDtypeStruct(shape, BF16)


def split(value):
    high = value.astype(BF16)
    return high, (value - high.astype(F32)).astype(BF16)


def split3(value):
    high = value.astype(BF16)
    rest = value - high.astype(F32)
    middle = rest.astype(BF16)
    return high, middle, (rest - middle.astype(F32)).astype(BF16)


def doubled(value):
    both = jnp.concatenate(split(value), axis=0)
    return jnp.concatenate([both, both], axis=1)


def apply(wide, stacked, dims=NN):
    rows = wide.shape[0] // 2
    both = lax.dot_general(wide, stacked, dims, preferred_element_type=F32)
    return both[:rows] + both[rows:]


def product(value, stacked, dims=NN):
    return apply(doubled(value), stacked, dims)


def stack_scalars(first, second):
    row = lax.broadcasted_iota(jnp.int32, (8, first[0].shape[1]), 0)
    block = jnp.zeros(row.shape, F32)
    for i, value in enumerate(first + second):
        block = jnp.where(row == i, value, block)
    return block


def features(scaled, unit):
    value = scaled * (1.0 / unit)
    whole = jnp.floor(value + 0.5)
    part = value - whole
    f1, f2, f3 = (f.astype(F32) for f in split3(part))
    norm = jnp.sum(whole * whole, axis=0, keepdims=True)
    rest = jnp.sum(part * (2.0 * whole + part), axis=0, keepdims=True)
    norms = [-f.astype(F32) for f in split3(norm)]
    rests = [-f.astype(F32) for f in split3(rest)]
    ones = [jnp.ones_like(norm)] * 3
    twice = 2.0 * whole
    g1, g2, g3 = 2.0 * f1, 2.0 * f2, 2.0 * f3
    left = (
        jnp.concatenate([twice, stack_scalars(norms, ones)], axis=0),
        jnp.concatenate(
            [twice, twice, twice, g1, g2, g3, g1, g1, g2, stack_scalars(rests, ones)], axis=0
        ),
    )
    right = (
        jnp.concatenate([whole, stack_scalars(ones, norms)], axis=0),
        jnp.concatenate(
            [f1, f2, f3, whole, whole, whole, f1, f2, f1, stack_scalars(ones, rests)], axis=0
        ),
    )
    return tuple(a.T.astype(BF16) for a in left), tuple(a.astype(BF16) for a in right)


def unit_of(scaled):
    peak = jnp.max(jnp.max(jnp.abs(scaled), axis=1, keepdims=True), axis=0, keepdims=True)
    return jnp.maximum(peak, 1e-6) * (1.0 / 128.0)


def gauss(left, right, unit):
    squared = lax.dot_general(left[0], right[0], NN, preferred_element_type=F32)
    squared = squared + lax.dot_general(left[1], right[1], NN, preferred_element_type=F32)
    return jnp.exp2(squared * (unit * unit))


def pick(table, chosen):
    rows, pool = table.shape
    hit = lax.broadcasted_iota(jnp.int32, (pool, chosen.shape[1]), 0) == chosen
    onehot = jnp.where(hit, 1.0, 0.0).astype(BF16)
    stacked = jnp.concatenate([t.astype(F32) for t in split3(table)], axis=0).astype(BF16)
    parts = lax.dot_general(stacked, onehot, NN, preferred_element_type=F32)
    return parts[:rows] + parts[rows : 2 * rows] + parts[2 * rows :]


def write_wide(message, top, value):
    rows = value.shape[0]
    for k in range(value.shape[1] // LANES):
        start = top + k * rows
        message[start : start + rows, :] = value[:, k * LANES : (k + 1) * LANES]


def read_wide(message, top, rows, rank):
    starts = [top + k * rows for k in range(rank // LANES)]
    return jnp.concatenate([message[start : start + rows, :] for start in starts], axis=1)


def dots_at(rows, rank):
    return rows * (rank // LANES)


def message_rows(rows, rank, coords):
    return dots_at(rows, rank) + 8 + (dots_at(8, rank) if coords else 0)


def to_rows(columns):
    rows = columns[0].shape[0]
    block = column_state(columns)
    if rows < LANES:
        block = jnp.concatenate([block, jnp.zeros((LANES - rows, LANES), F32)], axis=0)
    return block.T[:8]


def to_columns(block, rows):
    square = jnp.concatenate([block, jnp.zeros((120, 128), F32)], axis=0)
    return square.T[:rows]


def row_sum(value):
    return jnp.sum(value, axis=1, keepdims=True)


def setup_kernel(stages, total, anchors, *refs):
    sources, refs = refs[:6], refs[6:]
    message, rhs, la, lb, ra, rb, basis, chosen_out, params = refs[:9]
    pts, skel, keep, scales, noise, sems = refs[9:]
    targets = (pts, rhs, skel, keep, scales, noise)
    copies = [
        pltpu.make_async_copy(source, target, sems.at[i])
        for i, (source, target) in enumerate(zip(sources, targets))
    ]
    for copy in copies:
        copy.start()
    for i in (0, 2, 4):
        copies[i].wait()
    dims, count = pts.shape
    points = jnp.concatenate([pts[...], jnp.zeros((8 - dims, count), F32)], axis=0)
    row = lax.broadcasted_iota(jnp.int32, (8, dims), 0)
    lane = lax.broadcasted_iota(jnp.int32, (8, dims), 1)
    spread = jnp.broadcast_to(scales[...], (8, dims))
    length = row_sum(jnp.where(row == lane, spread, 0.0))
    valid = lax.broadcasted_iota(jnp.int32, (8, 1), 0) < dims
    inverse = SCALE / jnp.where(valid, length, 1.0)
    low_end = jnp.min(points, axis=1, keepdims=True)
    shift = low_end + 0.5 * (jnp.max(points, axis=1, keepdims=True) - low_end)
    chosen = pick(points, skel[...])
    rows = rhs.shape[0]
    rank = chosen.shape[1]
    dots = dots_at(rows, rank)
    write_wide(message, dots + 8, chosen)
    scaled = (points - shift) * inverse
    unit = unit_of(scaled)
    (la[...], lb[...]), (ra[...], rb[...]) = features(scaled, unit)
    _, own = features((chosen - shift) * inverse, unit)
    for i in range(count // STRIP):
        strip = slice(i * STRIP, (i + 1) * STRIP)
        high, low = split(gauss((la[strip, :], lb[strip, :]), own, unit))
        basis[strip, :] = high
        basis[count + i * STRIP : count + (i + 1) * STRIP, :] = low
    copies[1].wait()
    value = rhs[...]
    write_wide(message, 0, product(value, basis[...]))
    message[dots : dots + 8, :] = to_rows([row_sum(value * value)])
    copies[3].wait()
    copies[5].wait()
    params[...] = column_state(
        [inverse, shift, jnp.broadcast_to(noise[...], (8, 1)), jnp.broadcast_to(unit, (8, 1))]
    )
    number = lax.axis_index("leaf") * anchors + lax.axis_index("sub")
    slot = 0
    for base, bits in stages:
        for level in range(1, bits + 1):
            depth = base + level
            swap = (number >> (depth - 1)) & 1
            for p in range(1 << (bits - level)):
                heap = (1 << (total - depth)) - 1 + ((number >> depth) ^ p)
                row_chosen = keep[pl.ds(heap, 1), :]
                other = jnp.where(row_chosen < rank, row_chosen + rank, row_chosen - rank)
                chosen_out[slot : slot + 1, :] = jnp.where(swap == 1, other, row_chosen)
                slot += 1


def dense_kernel(start, la, lb, ra, rb, rhs, params, tie, stacked, near):
    size, width = la.shape[0], stacked.shape[1]
    unit = params[0:1, 3:4]

    def body(k, carry):
        top = pl.multiple_of(k * STRIP, STRIP)
        strip, below = pl.ds(top, STRIP), pl.ds(pl.multiple_of(size + top, STRIP), STRIP)
        left = la[strip, :], lb[strip, :]
        for j in range(0, width, BLOCK):
            cut = slice(start + j, start + j + BLOCK)
            high, low = split(gauss(left, (ra[:, cut], rb[:, cut]), unit))
            stacked[strip, j : j + BLOCK] = high
            stacked[below, j : j + BLOCK] = low
        return carry

    lax.fori_loop(0, size // STRIP, body, 0, unroll=True)
    value = rhs[...]
    here = value[:, start : start + width]
    near[...] = params[0:1, 2:3] * here + product(value, stacked[...])


def flip_kernel(basis, tie, out):
    size, rank = basis.shape[0] // 2, basis.shape[1]
    for part in range(2):
        for i in range(0, size, STRIP):
            strip = basis[part * size + i : part * size + i + STRIP, :]
            out[part * rank : (part + 1) * rank, i : i + STRIP] = strip.T


def levels_of(count):
    return count.bit_length() - 1


def tree_slots(count):
    slots = {}
    for level in range(1, levels_of(count) + 1):
        for p in range(count >> level):
            slots[level, p] = len(slots)
    return slots


def sweep_up(weights, transfer, couple, top, measured=True):
    count = len(weights)
    slots = tree_slots(count)
    own_terms = []
    energy = None
    for level in range(1, levels_of(count) + 1):
        parents = []
        for p in range(count >> level):
            slot = slots[level, p]
            first, second = weights[2 * p], weights[2 * p + 1]
            if couple is not None and (measured or p == 0):
                crossed = product(second, couple[slot])
                if p == 0:
                    own_terms.append(crossed)
                if measured:
                    term = row_sum(first * crossed)
                    energy = term if energy is None else energy + term
            parent = None
            if (level < levels_of(count) or top) and (measured or top or p > 0):
                joined = jnp.concatenate([first, second], axis=1)
                parent = product(joined, transfer[slot])
            parents.append(parent)
        weights = parents
    return weights, own_terms, None if energy is None else 2.0 * energy


def own_half(transfer, slot):
    rank = transfer.shape[2]
    return transfer[slot, :rank, :], transfer[slot, 2 * rank : 3 * rank, :]


def sweep_down(search, own_terms, transfer, count):
    slots = tree_slots(count)
    for level in range(levels_of(count), 0, -1):
        own = own_terms[level - 1]
        if search is not None:
            half = jnp.concatenate(own_half(transfer, slots[level, 0]), axis=1)
            own = own + product(search, half, NT)
        search = own
    return search


def build_tree(coords, picks, params, transfer, couple, nodes, top, partial=False):
    count = len(coords)
    slots = tree_slots(count)
    rank = coords[0].shape[1]
    inverse, shift = params[:, 0:1], params[:, 1:2]
    scaled = [(c - shift) * inverse for c in coords]
    unit = unit_of(jnp.concatenate(scaled, axis=1))
    sides = [features(c, unit) for c in scaled]
    for level in range(1, levels_of(count) + 1):
        parents, parent_sides = [], []
        for p in range(count >> level):
            slot = slots[level, p]
            if couple is not None and (p == 0 or not partial):
                high, low = split(gauss(sides[2 * p + 1][0], sides[2 * p][1], unit))
                couple[slot, :rank, :] = high
                couple[slot, rank:, :] = low
            if level == levels_of(count) and (not top or transfer is None):
                continue
            if picks is None:
                parent = nodes[slot]
            else:
                joined = jnp.concatenate([coords[2 * p], coords[2 * p + 1]], axis=1)
                parent = pick(joined, picks[slot : slot + 1, :])
                if nodes is not None:
                    nodes[slot] = parent
            parent_side = features((parent - shift) * inverse, unit)
            for side in range(0 if transfer is None else 1 if partial and p == 0 else 2):
                high, low = split(gauss(sides[2 * p + side][0], parent_side[1], unit))
                transfer[slot, side * rank : (side + 1) * rank, :] = high
                transfer[slot, (side + 2) * rank : (side + 3) * rank, :] = low
            parents.append(parent)
            parent_sides.append(parent_side)
        coords, sides = parents, parent_sides
    return coords


def add_dots(messages, rows, rank):
    dots = slice(dots_at(rows, rank), dots_at(rows, rank) + 8)
    total = messages[0][dots, :]
    for message in messages[1:]:
        total = total + message[dots, :]
    return total


def coords_of(messages, rows, rank):
    return [read_wide(m, dots_at(rows, rank) + 8, 8, rank) for m in messages]


def weights_of(messages, rows, rank):
    return [read_wide(m, 0, rows, rank) for m in messages]


def lower_first_kernel(rows, count, offset, refs):
    messages = refs[:count]
    params, chosen = refs[count : count + 2]
    message, transfer, nodes = refs[-3:]
    rank = transfer.shape[2]
    picks = chosen[offset : offset + count - 1, :]
    coords = coords_of(messages, rows, rank)
    coords = build_tree(coords, picks, params, transfer, None, nodes, True)
    weights = weights_of(messages, rows, rank)
    weights, _, _ = sweep_up(weights, transfer, None, True)
    write_wide(message, 0, weights[0])
    dots = dots_at(rows, rank)
    message[dots : dots + 8, :] = add_dots(messages, rows, rank)
    write_wide(message, dots + 8, coords[0])


def lower_rest_kernel(rows, count, refs):
    messages = refs[:count]
    params, transfer, nodes, couple, terms = refs[count:]
    rank = couple.shape[2]
    coords = coords_of(messages, rows, rank)
    build_tree(coords, None, params, None, couple, nodes, False)
    weights = weights_of(messages, rows, rank)
    _, own_terms, _ = sweep_up(weights, transfer, couple, False, measured=False)
    for i, term in enumerate(own_terms):
        terms[i] = term


def lower_finish(rows, messages, message, terms, transfer, couple, top):
    rank = couple.shape[2]
    weights = weights_of(messages, rows, rank)
    weights, own_terms, energy = sweep_up(weights, transfer, couple, top)
    for i, term in enumerate(own_terms):
        terms[i] = term
    write_wide(message, 0, weights[0])
    dots = dots_at(rows, rank)
    extra = to_rows([jnp.zeros_like(energy)] * 7 + [energy])
    message[dots : dots + 8, :] = add_dots(messages, rows, rank) + extra


def lower_kernel(rows, count, top, refs):
    transfer, couple, message, terms = refs[count:]
    lower_finish(rows, refs[:count], message, terms, transfer, couple, top)


def upper_build(rows, count, offset, partial, refs):
    params, chosen = refs[count : count + 2]
    transfer, couple = refs[-2:]
    coords = coords_of(refs[:count], rows, couple.shape[2])
    picks = chosen[offset : offset + count - 1, :]
    build_tree(coords, picks, params, transfer, couple, None, False, partial)


def compose_kernel(counts, refs):
    out = refs[-1]
    halves = []
    for transfer, count in zip(refs, counts):
        slots = tree_slots(count)
        halves += [own_half(transfer, slots[i, 0]) for i in range(1, levels_of(count) + 1)]
    halves = halves[:-1]
    rank = out.shape[1]
    high, low = halves[0]
    for i, half in enumerate(halves):
        if i:
            chained = high.astype(F32) + low.astype(F32)
            high, low = split(product(chained, jnp.concatenate(half, axis=0)))
        out[i * rank : (i + 1) * rank, :] = high.T
        out[(len(halves) + i) * rank : (len(halves) + i + 1) * rank, :] = low.T


def far_search(rows, messages, upper, lower):
    transfer, couple = upper
    rank = couple.shape[2]
    weights = weights_of(messages, rows, rank)
    _, own_terms, _ = sweep_up(weights, transfer, couple, False, measured=False)
    search = sweep_down(None, own_terms, transfer, len(messages))
    for terms, below_transfer in reversed(lower):
        depth = terms.shape[0]
        below = [terms[i] for i in range(depth)]
        search = sweep_down(search, below, below_transfer, 1 << depth)
    size = sum(row_sum(w * w) for w in weights)
    return search, to_columns(add_dots(messages, rows, rank), rows), size


def far_field(rows, messages, upper, lower, path):
    transfer, couple = upper
    rank = couple.shape[2]
    weights = weights_of(messages, rows, rank)
    _, own_terms, energy = sweep_up(weights, transfer, couple, False)
    sums = to_columns(add_dots(messages, rows, rank), rows)
    below = [terms[i] for terms in lower for i in range(terms.shape[0])]
    search, *above = below + own_terms
    search = search + product(jnp.concatenate(above, axis=1), path[...])
    return search, sums, sums[:, 7:8] + energy


def near_field(wide, value, params, parts):
    cuts = [apply(wide, part[...]) for part in parts]
    return params[0:1, 2:3] * value + jnp.concatenate(cuts, axis=1)


def column_state(columns):
    rows = columns[0].shape[0]
    lane = lax.broadcasted_iota(jnp.int32, (rows, 128), 1)
    block = jnp.zeros((rows, 128), F32)
    for i, column in enumerate(columns):
        block = jnp.where(lane == i, column, block)
    return block


def take_refs(refs, *sizes):
    groups = []
    position = 0
    for size in sizes:
        groups.append(refs[position : position + size])
        position += size
    groups.append(refs[position:])
    return groups


def open_refs(rows, count, stages, refs):
    messages, lower, upper, basis, rest = take_refs(refs, count, 2 * stages, 2, 2)
    lower = [lower[i : i + 2] for i in range(0, 2 * stages, 2)]
    return far_search(rows, messages, upper, lower), basis, rest


def open_composed(rows, count, stages, refs):
    messages, terms, upper, path, basis, rest = take_refs(refs, count, stages, 2, 1, 2)
    return far_field(rows, messages, upper, terms, path[0]), basis, rest


def first_kernel(rows, count, stages, parts, refs):
    (search, sums, size), basis, rest = open_refs(rows, count, stages, refs)
    dense, rest = take_refs(rest, parts)
    params, rhs = rest[:2]
    near_parts, (message, q_out, near_out, state) = take_refs(rest[2:], parts)
    near_b = jnp.concatenate([n[...] for n in near_parts], axis=1)
    norm = sums[:, 0:1]
    rate = norm / (params[0:1, 2:3] * norm + size)
    q = rate * (near_b + product(search, basis[1][...]))
    q_out[...] = q
    wide = doubled(q)
    write_wide(message, 0, apply(wide, basis[0][...]))
    near_q = near_field(wide, q, params, dense)
    near_out[...] = near_q
    dots = [row_sum(rhs[...] * q), row_sum(q * q), row_sum(q * near_q)]
    message[message.shape[0] - 8 :, :] = to_rows(dots)
    state[...] = column_state([norm, rate])


def second_kernel(rows, count, stages, parts, refs):
    (search, sums, far), basis, rest = open_composed(rows, count, stages, refs)
    dense, rest = take_refs(rest, parts)
    params, rhs, q_in, near_in, state_in = rest[:5]
    message, r_out, q_out, near_out, state = rest[5:]
    norm0, rate = state_in[:, 0:1], state_in[:, 1:2]
    bq, qq, qaq = sums[:, 0:1], sums[:, 1:2], sums[:, 2:3] + far
    step = norm0 / bq
    alpha0 = step * rate
    norm1 = step * step * qq - norm0
    beta = norm1 / norm0
    back = 1.0 / rate
    rhs_v, q = rhs[...], q_in[...]
    r1 = rhs_v - step * q
    q0 = back * q
    aq = near_in[...] + product(search, basis[1][...])
    q1 = (1.0 + beta) * q0 - step * aq
    rar = back * (bq - 2.0 * step * qq) + step * step * qaq
    cross = back * (bq - step * qq)
    curve = rar + 2.0 * beta * cross + beta * beta * (back * bq)
    alpha1 = norm1 / curve
    r2 = r1 - alpha1 * q1
    r_out[...] = r2
    q_out[...] = q1
    wide = doubled(r2)
    write_wide(message, 0, apply(wide, basis[0][...]))
    near = near_field(wide, r2, params, dense)
    near_out[...] = near
    dots = [row_sum(r2 * r2), row_sum(r2 * q1), row_sum(r2 * near)]
    message[message.shape[0] - 8 :, :] = to_rows(dots)
    state[...] = column_state([norm1, curve, alpha0, alpha1, step, beta])


def update_kernel(rhs, q, state, x_out, d_out):
    alpha0, alpha1, step, beta = (state[:, i : i + 1] for i in range(2, 6))
    rhs_v = rhs[...]
    d1 = rhs_v - step * q[...] + beta * rhs_v
    d_out[...] = d1
    x_out[...] = alpha0 * rhs_v + alpha1 * d1


def last_kernel(rows, count, stages, refs):
    (search, sums, far), basis, rest = open_composed(rows, count, stages, refs)
    x_in, r_in, d_in, q_in, near_in, state_in, x_out, r_out, x_done, r_done, sems = rest
    norm1, curve1 = state_in[:, 0:1], state_in[:, 1:2]
    norm2, cross, rar = sums[:, 0:1], sums[:, 1:2], sums[:, 2:3] + far
    beta = norm2 / norm1
    curve = rar + 2.0 * beta * cross + beta * beta * curve1
    alpha = norm2 / curve
    r2 = r_in[...]
    x_done[...] = x_in[...] + alpha * (r2 + beta * d_in[...])
    x_copy = pltpu.make_async_copy(x_done, x_out, sems.at[0])
    x_copy.start()
    image = near_in[...] + product(search, basis[1][...]) + beta * q_in[...]
    r_done[...] = r2 - alpha * image
    r_copy = pltpu.make_async_copy(r_done, r_out, sems.at[1])
    r_copy.start()
    x_copy.wait()
    r_copy.wait()


def gather(value, stage):
    axis, shift, bits = stage
    size = lax.axis_size(axis)
    pairs = [[(i, i ^ (s << shift)) for i in range(size)] for s in range(1, 1 << bits)]
    return [value] + [lax.ppermute(value, axis, pair) for pair in pairs]


def refs_of(kernel, *args):
    return lambda *refs: kernel(*args, refs)


def body(points, targets, leaf_skel, node_keep, lengthscales, noise_var):
    dims, size = points.shape
    rows = targets.shape[0]
    rank = leaf_skel.shape[1]
    subs = lax.axis_size("sub")
    stages = []
    total = 0
    for axis in ("sub", "leaf"):
        axis_bits = levels_of(lax.axis_size(axis))
        for shift in range(0, axis_bits, 3):
            bits = min(3, axis_bits - shift)
            stages.append((total + shift, axis, shift, bits))
        total += axis_bits
    bases = tuple((base, bits) for base, _, _, bits in stages)
    hops = [stage[1:] for stage in stages]
    counts = [1 << bits for _, bits in bases]
    slots = sum(counts) - len(counts)
    offsets = [sum(counts[:i]) - i for i in range(len(counts))]
    stage_count = len(stages) - 1

    message, rhs, la, lb, ra, rb, basis, chosen, params = call(
        functools.partial(setup_kernel, bases, total, subs),
        [
            f32_shape(message_rows(rows, rank, True), LANES),
            f32_shape(rows, size),
            bf16_shape(size, 16),
            bf16_shape(size, 80),
            bf16_shape(16, size),
            bf16_shape(80, size),
            bf16_shape(2 * size, rank),
            jax.ShapeDtypeStruct((slots, rank), jnp.int32),
            f32_shape(8, 128),
        ],
        [
            points,
            targets,
            leaf_skel,
            node_keep,
            jnp.reshape(lengthscales, (1, dims)),
            jnp.reshape(noise_var, (1, 1)),
        ],
        anywhere=range(6),
        pinned=range(5),
        scratch=[
            pltpu.VMEM((dims, size), F32),
            pltpu.VMEM((1, rank), jnp.int32),
            pltpu.VMEM(node_keep.shape, jnp.int32),
            pltpu.VMEM((1, dims), F32),
            pltpu.VMEM((1, 1), F32),
            pltpu.SemaphoreType.DMA((6,)),
        ],
        name="setup",
    )

    def tree_shapes(count):
        nodes = count - 1
        return [bf16_shape(nodes, 4 * rank, rank), bf16_shape(nodes, 2 * rank, rank)]

    first_width = size // BLOCK * 3 // 8 * BLOCK
    widths = [first_width, size - first_width]
    dense, near_parts = [], []

    def build_dense(start, width, tie):
        stacked, near = call(
            functools.partial(dense_kernel, start),
            [resident_shape(2 * size, width), f32_shape(rows, width)],
            [la, lb, ra, rb, rhs, params, tie],
            cost=(6 * rows * size * width + 192 * size * width, size * width),
            name="dense",
        )
        dense.append(stacked)
        near_parts.append(near)

    trees, pending = [], []
    terms_all = []
    for i in range(stage_count):
        messages = gather(message, hops[i])
        extra = []
        if i == 0:
            build_dense(0, widths[0], params)
            extra = near_parts[:1]
        next_message, transfer, nodes = call(
            refs_of(lower_first_kernel, rows, counts[i], offsets[i]),
            [
                f32_shape(message_rows(rows, rank, True), LANES),
                tree_shapes(counts[i])[0],
                f32_shape(counts[i] - 1, 8, rank),
            ],
            messages + [params, chosen] + extra,
            name="lower_first",
        )
        pending.append((i, messages, transfer, nodes))
        message = next_message
    messages = gather(message, hops[-1])
    build_dense(widths[0], widths[1], message)
    (flipped,) = call(
        flip_kernel,
        [bf16_shape(2 * rank, size)],
        [basis, message],
        cost=(64 * size * rank, 0),
        name="flip",
    )
    basis = [basis, flipped]
    for i, arrived, transfer, nodes in pending:
        couple, terms = call(
            refs_of(lower_rest_kernel, rows, counts[i]),
            [tree_shapes(counts[i])[1], f32_shape(bases[i][1], rows, rank)],
            arrived + [params, transfer, nodes],
            cost=(48 * rank * rank * rank, rank * rank * counts[i]),
            name="lower_rest",
        )
        trees.append([transfer, couple])
        terms_all.append(terms)

    def build_upper(partial, extra):
        return call(
            refs_of(upper_build, rows, counts[-1], offsets[-1], partial),
            tree_shapes(counts[-1]),
            messages_first + [params, chosen] + extra,
            cost=None if partial else (48 * rank * rank * rank, rank * rank * counts[-1]),
            name="upper_build",
        )

    messages_first = messages
    upper = build_upper(True, [])

    state_shape = f32_shape(rows, 128)
    vector = f32_shape(rows, size)
    message_shape = f32_shape(message_rows(rows, rank, False), LANES)

    def lower_of(terms_all):
        return [a for terms, tree in zip(terms_all, trees) for a in (terms, tree[0])]

    def exchange(message, shadow=None):
        terms_all = []
        made = None
        for i in range(stage_count):
            messages = gather(message, hops[i])
            if i == 0 and shadow is not None:
                made = shadow()
            message, terms = call(
                refs_of(lower_kernel, rows, counts[i], True),
                [message_shape, f32_shape(bases[i][1], rows, rank)],
                messages + trees[i],
                name="lower",
            )
            terms_all.append(terms)
        return gather(message, hops[-1]) + terms_all, made

    fixed = (rows, counts[-1], stage_count)
    message, q, near, state = call(
        refs_of(first_kernel, *fixed, len(widths)),
        [message_shape, vector, vector, state_shape],
        messages + lower_of(terms_all) + upper + basis + dense + [params, rhs] + near_parts,
        resident=dense,
        name="first",
    )

    def compose():
        upper = build_upper(False, [state])
        pairs = [tree[0] for tree in trees + [upper]]
        path = call(
            refs_of(compose_kernel, counts),
            [bf16_shape(2 * (total - 1) * rank, rank)],
            pairs + [state],
            cost=(12 * rank * rank * rank, 0),
            name="compose",
        )
        return upper, path

    arrived, (upper, path) = exchange(message, compose)
    first_q = q
    message, r, q, near, state = call(
        refs_of(second_kernel, *fixed, len(widths)),
        [message_shape, vector, vector, vector, state_shape],
        arrived + upper + path + basis + dense + [params, rhs, q, near, state],
        resident=dense,
        name="second",
    )

    def update():
        return call(
            update_kernel,
            [vector, vector],
            [rhs, first_q, state],
            cost=(8 * rows * size, 0),
            name="update",
        )

    arrived, (x, d) = exchange(message, update)
    return tuple(
        call(
            refs_of(last_kernel, *fixed),
            [vector, vector],
            arrived + upper + path + basis + [x, r, d, q, near, state],
            copied=True,
            scratch=[
                pltpu.VMEM((rows, size), F32),
                pltpu.VMEM((rows, size), F32),
                pltpu.SemaphoreType.DMA((2,)),
            ],
            name="last",
        )
    )


def solution(mesh):
    in_specs = (
        P(None, ("parts", "leaf", "sub")),
        P(None, ("parts", "leaf", "sub")),
        P(("parts", "leaf", "sub"), None),
        P("parts", None),
        P("parts"),
        P("parts"),
    )
    out_specs = (P(None, ("parts", "leaf", "sub")), P(None, ("parts", "leaf", "sub")))
    return jax.shard_map(body, mesh=mesh, in_specs=in_specs, out_specs=out_specs, check_vma=False)
```

```python
import functools
import math

import jax
import jax.numpy as jnp
from jax import lax
from jax.experimental import pallas as pl
from jax.experimental.pallas import tpu as pltpu
from jax.sharding import PartitionSpec as P

F32 = jnp.float32
BF16 = jnp.bfloat16
VMEM = pl.BlockSpec(memory_space=pltpu.VMEM)
ANY = pl.BlockSpec(memory_space=pl.ANY)
HBM = pltpu.MemorySpace.HBM
NN = (((1,), (0,)), ((), ()))
NT = (((1,), (1,)), ((), ()))
SCALE = math.sqrt(0.5 * math.log2(math.e))
STRIP = 256
LANES = 128
BLOCK = 256


def resident_shape(*shape):
    return pltpu.VMEM(shape, BF16)


def is_resident(shape):
    return not isinstance(shape, jax.ShapeDtypeStruct)


def call(kernel, out_shape, args, anywhere=(), pinned=(), resident=(), copied=False, scratch=(), name=None, cost=None):
    total = sum(a.size * a.dtype.itemsize for i, a in enumerate(args) if i not in anywhere)
    total += sum(math.prod(s.shape) * s.dtype.itemsize for s in out_shape)
    held = sum(a.size * a.dtype.itemsize for a in args if any(a is kept for kept in resident))
    held += sum(math.prod(s.shape) * s.dtype.itemsize for s in out_shape if is_resident(s))
    if cost is not None:
        cost = pl.CostEstimate(flops=cost[0], transcendentals=cost[1], bytes_accessed=total)
    args = [
        pltpu.with_memory_space_constraint(a, HBM) if i in pinned else a for i, a in enumerate(args)
    ]
    results = pl.pallas_call(
        kernel,
        out_shape=list(out_shape),
        in_specs=[ANY if i in anywhere else VMEM for i in range(len(args))],
        out_specs=[ANY if copied else VMEM] * len(out_shape),
        scratch_shapes=list(scratch),
        compiler_params=pltpu.CompilerParams(vmem_limit_bytes=total - held + (6 << 20)),
        cost_estimate=cost,
        name=name,
    )(*args)
    return list(results)


def f32_shape(*shape):
    return jax.ShapeDtypeStruct(shape, F32)


def bf16_shape(*shape):
    return jax.ShapeDtypeStruct(shape, BF16)


def split(value):
    high = value.astype(BF16)
    return high, (value - high.astype(F32)).astype(BF16)


def split3(value):
    high = value.astype(BF16)
    rest = value - high.astype(F32)
    middle = rest.astype(BF16)
    return high, middle, (rest - middle.astype(F32)).astype(BF16)


def doubled(value):
    both = jnp.concatenate(split(value), axis=0)
    return jnp.concatenate([both, both], axis=1)


def apply(wide, stacked, dims=NN):
    rows = wide.shape[0] // 2
    both = lax.dot_general(wide, stacked, dims, preferred_element_type=F32)
    return both[:rows] + both[rows:]


def product(value, stacked, dims=NN):
    return apply(doubled(value), stacked, dims)


def stack_scalars(first, second):
    row = lax.broadcasted_iota(jnp.int32, (8, first[0].shape[1]), 0)
    block = jnp.zeros(row.shape, F32)
    for i, value in enumerate(first + second):
        block = jnp.where(row == i, value, block)
    return block


def features(scaled, unit):
    value = scaled * (1.0 / unit)
    whole = jnp.floor(value + 0.5)
    part = value - whole
    f1, f2, f3 = (f.astype(F32) for f in split3(part))
    norm = jnp.sum(whole * whole, axis=0, keepdims=True)
    rest = jnp.sum(part * (2.0 * whole + part), axis=0, keepdims=True)
    norms = [-f.astype(F32) for f in split3(norm)]
    rests = [-f.astype(F32) for f in split3(rest)]
    ones = [jnp.ones_like(norm)] * 3
    twice = 2.0 * whole
    g1, g2, g3 = 2.0 * f1, 2.0 * f2, 2.0 * f3
    left = (
        jnp.concatenate([twice, stack_scalars(norms, ones)], axis=0),
        jnp.concatenate(
            [twice, twice, twice, g1, g2, g3, g1, g1, g2, stack_scalars(rests, ones)], axis=0
        ),
    )
    right = (
        jnp.concatenate([whole, stack_scalars(ones, norms)], axis=0),
        jnp.concatenate(
            [f1, f2, f3, whole, whole, whole, f1, f2, f1, stack_scalars(ones, rests)], axis=0
        ),
    )
    return tuple(a.T.astype(BF16) for a in left), tuple(a.astype(BF16) for a in right)


def unit_of(scaled):
    peak = jnp.max(jnp.max(jnp.abs(scaled), axis=1, keepdims=True), axis=0, keepdims=True)
    return jnp.maximum(peak, 1e-6) * (1.0 / 128.0)


def gauss(left, right, unit):
    squared = lax.dot_general(left[0], right[0], NN, preferred_element_type=F32)
    squared = squared + lax.dot_general(left[1], right[1], NN, preferred_element_type=F32)
    return jnp.exp2(squared * (unit * unit))


def pick(table, chosen):
    rows, pool = table.shape
    hit = lax.broadcasted_iota(jnp.int32, (pool, chosen.shape[1]), 0) == chosen
    onehot = jnp.where(hit, 1.0, 0.0).astype(BF16)
    stacked = jnp.concatenate([t.astype(F32) for t in split3(table)], axis=0).astype(BF16)
    parts = lax.dot_general(stacked, onehot, NN, preferred_element_type=F32)
    return parts[:rows] + parts[rows : 2 * rows] + parts[2 * rows :]


def write_wide(message, top, value):
    rows = value.shape[0]
    for k in range(value.shape[1] // LANES):
        start = top + k * rows
        message[start : start + rows, :] = value[:, k * LANES : (k + 1) * LANES]


def read_wide(message, top, rows, rank):
    starts = [top + k * rows for k in range(rank // LANES)]
    return jnp.concatenate([message[start : start + rows, :] for start in starts], axis=1)


def dots_at(rows, rank):
    return rows * (rank // LANES)


def message_rows(rows, rank, coords):
    return dots_at(rows, rank) + 8 + (dots_at(8, rank) if coords else 0)


def to_rows(columns):
    rows = columns[0].shape[0]
    block = column_state(columns)
    if rows < LANES:
        block = jnp.concatenate([block, jnp.zeros((LANES - rows, LANES), F32)], axis=0)
    return block.T[:8]


def to_columns(block, rows):
    square = jnp.concatenate([block, jnp.zeros((120, 128), F32)], axis=0)
    return square.T[:rows]


def row_sum(value):
    return jnp.sum(value, axis=1, keepdims=True)


def setup_kernel(stages, total, anchors, *refs):
    sources, refs = refs[:6], refs[6:]
    message, rhs, la, lb, moved, basis, chosen_out, params = refs[:8]
    pts, skel, keep, scales, noise, sems = refs[8:]
    targets = (pts, rhs, skel, keep, scales, noise)
    copies = [
        pltpu.make_async_copy(source, target, sems.at[i])
        for i, (source, target) in enumerate(zip(sources, targets))
    ]
    for copy in copies:
        copy.start()
    for i in (0, 2, 4):
        copies[i].wait()
    dims, count = pts.shape
    points = jnp.concatenate([pts[...], jnp.zeros((8 - dims, count), F32)], axis=0)
    row = lax.broadcasted_iota(jnp.int32, (8, dims), 0)
    lane = lax.broadcasted_iota(jnp.int32, (8, dims), 1)
    spread = jnp.broadcast_to(scales[...], (8, dims))
    length = row_sum(jnp.where(row == lane, spread, 0.0))
    valid = lax.broadcasted_iota(jnp.int32, (8, 1), 0) < dims
    inverse = SCALE / jnp.where(valid, length, 1.0)
    low_end = jnp.min(points, axis=1, keepdims=True)
    shift = low_end + 0.5 * (jnp.max(points, axis=1, keepdims=True) - low_end)
    chosen = pick(points, skel[...])
    rows = rhs.shape[0]
    rank = chosen.shape[1]
    dots = dots_at(rows, rank)
    write_wide(message, dots + 8, chosen)
    scaled = (points - shift) * inverse
    unit = unit_of(scaled)
    moved[...] = scaled
    (la[...], lb[...]), _ = features(scaled, unit)
    _, own = features((chosen - shift) * inverse, unit)
    for i in range(count // STRIP):
        strip = slice(i * STRIP, (i + 1) * STRIP)
        high, low = split(gauss((la[strip, :], lb[strip, :]), own, unit))
        basis[strip, :] = high
        basis[count + i * STRIP : count + (i + 1) * STRIP, :] = low
    copies[1].wait()
    value = rhs[...]
    write_wide(message, 0, product(value, basis[...]))
    message[dots : dots + 8, :] = to_rows([row_sum(value * value)])
    copies[3].wait()
    copies[5].wait()
    params[...] = column_state(
        [inverse, shift, jnp.broadcast_to(noise[...], (8, 1)), jnp.broadcast_to(unit, (8, 1))]
    )
    number = lax.axis_index("leaf") * anchors + lax.axis_index("sub")
    slot = 0
    for base, bits in stages:
        for level in range(1, bits + 1):
            depth = base + level
            swap = (number >> (depth - 1)) & 1
            for p in range(1 << (bits - level)):
                heap = (1 << (total - depth)) - 1 + ((number >> depth) ^ p)
                row_chosen = keep[pl.ds(heap, 1), :]
                other = jnp.where(row_chosen < rank, row_chosen + rank, row_chosen - rank)
                chosen_out[slot : slot + 1, :] = jnp.where(swap == 1, other, row_chosen)
                slot += 1


def dense_kernel(start, la, lb, moved, rhs, params, tie, stacked, near):
    size, width = la.shape[0], stacked.shape[1]
    unit = params[0:1, 3:4]
    _, (ra, rb) = features(moved[:, start : start + width], unit)

    def body(k, carry):
        top = pl.multiple_of(k * STRIP, STRIP)
        strip, below = pl.ds(top, STRIP), pl.ds(pl.multiple_of(size + top, STRIP), STRIP)
        left = la[strip, :], lb[strip, :]
        for j in range(0, width, BLOCK):
            cut = slice(j, j + BLOCK)
            high, low = split(gauss(left, (ra[:, cut], rb[:, cut]), unit))
            stacked[strip, j : j + BLOCK] = high
            stacked[below, j : j + BLOCK] = low
        return carry

    lax.fori_loop(0, size // STRIP, body, 0, unroll=True)
    value = rhs[...]
    here = value[:, start : start + width]
    near[...] = params[0:1, 2:3] * here + product(value, stacked[...])


def flip_kernel(basis, tie, out):
    size, rank = basis.shape[0] // 2, basis.shape[1]
    for part in range(2):
        for i in range(0, size, STRIP):
            strip = basis[part * size + i : part * size + i + STRIP, :]
            out[part * rank : (part + 1) * rank, i : i + STRIP] = strip.T


def levels_of(count):
    return count.bit_length() - 1


def tree_slots(count):
    slots = {}
    for level in range(1, levels_of(count) + 1):
        for p in range(count >> level):
            slots[level, p] = len(slots)
    return slots


def sweep_up(weights, transfer, couple, top, measured=True):
    count = len(weights)
    slots = tree_slots(count)
    own_terms = []
    energy = None
    for level in range(1, levels_of(count) + 1):
        parents = []
        for p in range(count >> level):
            slot = slots[level, p]
            first, second = weights[2 * p], weights[2 * p + 1]
            if couple is not None and (measured or p == 0):
                crossed = product(second, couple[slot])
                if p == 0:
                    own_terms.append(crossed)
                if measured:
                    term = row_sum(first * crossed)
                    energy = term if energy is None else energy + term
            parent = None
            if (level < levels_of(count) or top) and (measured or top or p > 0):
                joined = jnp.concatenate([first, second], axis=1)
                parent = product(joined, transfer[slot])
            parents.append(parent)
        weights = parents
    return weights, own_terms, None if energy is None else 2.0 * energy


def own_half(transfer, slot):
    rank = transfer.shape[2]
    return transfer[slot, :rank, :], transfer[slot, 2 * rank : 3 * rank, :]


def sweep_down(search, own_terms, transfer, count):
    slots = tree_slots(count)
    for level in range(levels_of(count), 0, -1):
        own = own_terms[level - 1]
        if search is not None:
            half = jnp.concatenate(own_half(transfer, slots[level, 0]), axis=1)
            own = own + product(search, half, NT)
        search = own
    return search


def build_tree(coords, picks, params, transfer, couple, nodes, top, partial=False):
    count = len(coords)
    slots = tree_slots(count)
    rank = coords[0].shape[1]
    inverse, shift = params[:, 0:1], params[:, 1:2]
    scaled = [(c - shift) * inverse for c in coords]
    unit = unit_of(jnp.concatenate(scaled, axis=1))
    sides = [features(c, unit) for c in scaled]
    for level in range(1, levels_of(count) + 1):
        parents, parent_sides = [], []
        for p in range(count >> level):
            slot = slots[level, p]
            if couple is not None and (p == 0 or not partial):
                high, low = split(gauss(sides[2 * p + 1][0], sides[2 * p][1], unit))
                couple[slot, :rank, :] = high
                couple[slot, rank:, :] = low
            if level == levels_of(count) and (not top or transfer is None):
                continue
            if picks is None:
                parent = nodes[slot]
            else:
                joined = jnp.concatenate([coords[2 * p], coords[2 * p + 1]], axis=1)
                parent = pick(joined, picks[slot : slot + 1, :])
                if nodes is not None:
                    nodes[slot] = parent
            parent_side = features((parent - shift) * inverse, unit)
            for side in range(0 if transfer is None else 1 if partial and p == 0 else 2):
                high, low = split(gauss(sides[2 * p + side][0], parent_side[1], unit))
                transfer[slot, side * rank : (side + 1) * rank, :] = high
                transfer[slot, (side + 2) * rank : (side + 3) * rank, :] = low
            parents.append(parent)
            parent_sides.append(parent_side)
        coords, sides = parents, parent_sides
    return coords


def add_dots(messages, rows, rank):
    dots = slice(dots_at(rows, rank), dots_at(rows, rank) + 8)
    total = messages[0][dots, :]
    for message in messages[1:]:
        total = total + message[dots, :]
    return total


def coords_of(messages, rows, rank):
    return [read_wide(m, dots_at(rows, rank) + 8, 8, rank) for m in messages]


def weights_of(messages, rows, rank):
    return [read_wide(m, 0, rows, rank) for m in messages]


def lower_first_kernel(rows, count, offset, refs):
    messages = refs[:count]
    params, chosen = refs[count : count + 2]
    message, transfer, nodes = refs[-3:]
    rank = transfer.shape[2]
    picks = chosen[offset : offset + count - 1, :]
    coords = coords_of(messages, rows, rank)
    coords = build_tree(coords, picks, params, transfer, None, nodes, True)
    weights = weights_of(messages, rows, rank)
    weights, _, _ = sweep_up(weights, transfer, None, True)
    write_wide(message, 0, weights[0])
    dots = dots_at(rows, rank)
    message[dots : dots + 8, :] = add_dots(messages, rows, rank)
    write_wide(message, dots + 8, coords[0])


def lower_rest_kernel(rows, count, refs):
    messages = refs[:count]
    params, transfer, nodes, couple, terms = refs[count:]
    rank = couple.shape[2]
    coords = coords_of(messages, rows, rank)
    build_tree(coords, None, params, None, couple, nodes, False)
    weights = weights_of(messages, rows, rank)
    _, own_terms, _ = sweep_up(weights, transfer, couple, False, measured=False)
    for i, term in enumerate(own_terms):
        terms[i] = term


def lower_finish(rows, messages, message, terms, transfer, couple, top):
    rank = couple.shape[2]
    weights = weights_of(messages, rows, rank)
    weights, own_terms, energy = sweep_up(weights, transfer, couple, top)
    for i, term in enumerate(own_terms):
        terms[i] = term
    write_wide(message, 0, weights[0])
    dots = dots_at(rows, rank)
    extra = to_rows([jnp.zeros_like(energy)] * 7 + [energy])
    message[dots : dots + 8, :] = add_dots(messages, rows, rank) + extra


def lower_kernel(rows, count, top, refs):
    transfer, couple, message, terms = refs[count:]
    lower_finish(rows, refs[:count], message, terms, transfer, couple, top)


def upper_build(rows, count, offset, partial, refs):
    params, chosen = refs[count : count + 2]
    transfer, couple = refs[-2:]
    coords = coords_of(refs[:count], rows, couple.shape[2])
    picks = chosen[offset : offset + count - 1, :]
    build_tree(coords, picks, params, transfer, couple, None, False, partial)


def compose_kernel(counts, refs):
    out = refs[-1]
    halves = []
    for transfer, count in zip(refs, counts):
        slots = tree_slots(count)
        halves += [own_half(transfer, slots[i, 0]) for i in range(1, levels_of(count) + 1)]
    halves = halves[:-1]
    rank = out.shape[1]
    high, low = halves[0]
    for i, half in enumerate(halves):
        if i:
            chained = high.astype(F32) + low.astype(F32)
            high, low = split(product(chained, jnp.concatenate(half, axis=0)))
        out[i * rank : (i + 1) * rank, :] = high.T
        out[(len(halves) + i) * rank : (len(halves) + i + 1) * rank, :] = low.T


def far_search(rows, messages, upper, lower):
    transfer, couple = upper
    rank = couple.shape[2]
    weights = weights_of(messages, rows, rank)
    _, own_terms, _ = sweep_up(weights, transfer, couple, False, measured=False)
    search = sweep_down(None, own_terms, transfer, len(messages))
    for terms, below_transfer in reversed(lower):
        depth = terms.shape[0]
        below = [terms[i] for i in range(depth)]
        search = sweep_down(search, below, below_transfer, 1 << depth)
    size = sum(row_sum(w * w) for w in weights)
    return search, to_columns(add_dots(messages, rows, rank), rows), size


def far_field(rows, messages, upper, lower, path):
    transfer, couple = upper
    rank = couple.shape[2]
    weights = weights_of(messages, rows, rank)
    _, own_terms, energy = sweep_up(weights, transfer, couple, False)
    sums = to_columns(add_dots(messages, rows, rank), rows)
    below = [terms[i] for terms in lower for i in range(terms.shape[0])]
    search, *above = below + own_terms
    search = search + product(jnp.concatenate(above, axis=1), path[...])
    return search, sums, sums[:, 7:8] + energy


def near_field(wide, value, params, parts):
    cuts = [apply(wide, part[...]) for part in parts]
    return params[0:1, 2:3] * value + jnp.concatenate(cuts, axis=1)


def column_state(columns):
    rows = columns[0].shape[0]
    lane = lax.broadcasted_iota(jnp.int32, (rows, 128), 1)
    block = jnp.zeros((rows, 128), F32)
    for i, column in enumerate(columns):
        block = jnp.where(lane == i, column, block)
    return block


def take_refs(refs, *sizes):
    groups = []
    position = 0
    for size in sizes:
        groups.append(refs[position : position + size])
        position += size
    groups.append(refs[position:])
    return groups


def open_refs(rows, count, stages, refs):
    messages, lower, upper, basis, rest = take_refs(refs, count, 2 * stages, 2, 2)
    lower = [lower[i : i + 2] for i in range(0, 2 * stages, 2)]
    return far_search(rows, messages, upper, lower), basis, rest


def open_composed(rows, count, stages, refs):
    messages, terms, upper, path, basis, rest = take_refs(refs, count, stages, 2, 1, 2)
    return far_field(rows, messages, upper, terms, path[0]), basis, rest


def first_kernel(rows, count, stages, parts, refs):
    (search, sums, size), basis, rest = open_refs(rows, count, stages, refs)
    dense, rest = take_refs(rest, parts)
    params, rhs = rest[:2]
    near_parts, (message, q_out, near_out, state) = take_refs(rest[2:], parts)
    near_b = jnp.concatenate([n[...] for n in near_parts], axis=1)
    norm = sums[:, 0:1]
    rate = norm / (params[0:1, 2:3] * norm + size)
    q = rate * (near_b + product(search, basis[1][...]))
    q_out[...] = q
    wide = doubled(q)
    write_wide(message, 0, apply(wide, basis[0][...]))
    near_q = near_field(wide, q, params, dense)
    near_out[...] = near_q
    dots = [row_sum(rhs[...] * q), row_sum(q * q), row_sum(q * near_q)]
    message[message.shape[0] - 8 :, :] = to_rows(dots)
    state[...] = column_state([norm, rate])


def second_kernel(rows, count, stages, parts, refs):
    (search, sums, far), basis, rest = open_composed(rows, count, stages, refs)
    dense, rest = take_refs(rest, parts)
    params, rhs, q_in, near_in, state_in = rest[:5]
    message, r_out, q_out, near_out, state = rest[5:]
    norm0, rate = state_in[:, 0:1], state_in[:, 1:2]
    bq, qq, qaq = sums[:, 0:1], sums[:, 1:2], sums[:, 2:3] + far
    step = norm0 / bq
    alpha0 = step * rate
    norm1 = step * step * qq - norm0
    beta = norm1 / norm0
    back = 1.0 / rate
    rhs_v, q = rhs[...], q_in[...]
    r1 = rhs_v - step * q
    q0 = back * q
    aq = near_in[...] + product(search, basis[1][...])
    q1 = (1.0 + beta) * q0 - step * aq
    rar = back * (bq - 2.0 * step * qq) + step * step * qaq
    cross = back * (bq - step * qq)
    curve = rar + 2.0 * beta * cross + beta * beta * (back * bq)
    alpha1 = norm1 / curve
    r2 = r1 - alpha1 * q1
    r_out[...] = r2
    q_out[...] = q1
    wide = doubled(r2)
    write_wide(message, 0, apply(wide, basis[0][...]))
    near = near_field(wide, r2, params, dense)
    near_out[...] = near
    dots = [row_sum(r2 * r2), row_sum(r2 * q1), row_sum(r2 * near)]
    message[message.shape[0] - 8 :, :] = to_rows(dots)
    state[...] = column_state([norm1, curve, alpha0, alpha1, step, beta])


def update_kernel(rhs, q, state, x_out, d_out):
    alpha0, alpha1, step, beta = (state[:, i : i + 1] for i in range(2, 6))
    rhs_v = rhs[...]
    d1 = rhs_v - step * q[...] + beta * rhs_v
    d_out[...] = d1
    x_out[...] = alpha0 * rhs_v + alpha1 * d1


def last_kernel(rows, count, stages, refs):
    (search, sums, far), basis, rest = open_composed(rows, count, stages, refs)
    x_in, r_in, d_in, q_in, near_in, state_in, x_out, r_out, x_done, r_done, sems = rest
    norm1, curve1 = state_in[:, 0:1], state_in[:, 1:2]
    norm2, cross, rar = sums[:, 0:1], sums[:, 1:2], sums[:, 2:3] + far
    beta = norm2 / norm1
    curve = rar + 2.0 * beta * cross + beta * beta * curve1
    alpha = norm2 / curve
    r2 = r_in[...]
    x_done[...] = x_in[...] + alpha * (r2 + beta * d_in[...])
    x_copy = pltpu.make_async_copy(x_done, x_out, sems.at[0])
    x_copy.start()
    image = near_in[...] + product(search, basis[1][...]) + beta * q_in[...]
    r_done[...] = r2 - alpha * image
    r_copy = pltpu.make_async_copy(r_done, r_out, sems.at[1])
    r_copy.start()
    x_copy.wait()
    r_copy.wait()


def gather(value, stage):
    axis, shift, bits = stage
    size = lax.axis_size(axis)
    pairs = [[(i, i ^ (s << shift)) for i in range(size)] for s in range(1, 1 << bits)]
    return [value] + [lax.ppermute(value, axis, pair) for pair in pairs]


def refs_of(kernel, *args):
    return lambda *refs: kernel(*args, refs)


def body(points, targets, leaf_skel, node_keep, lengthscales, noise_var):
    dims, size = points.shape
    rows = targets.shape[0]
    rank = leaf_skel.shape[1]
    subs = lax.axis_size("sub")
    stages = []
    total = 0
    for axis in ("sub", "leaf"):
        axis_bits = levels_of(lax.axis_size(axis))
        for shift in range(0, axis_bits, 3):
            bits = min(3, axis_bits - shift)
            stages.append((total + shift, axis, shift, bits))
        total += axis_bits
    bases = tuple((base, bits) for base, _, _, bits in stages)
    hops = [stage[1:] for stage in stages]
    counts = [1 << bits for _, bits in bases]
    slots = sum(counts) - len(counts)
    offsets = [sum(counts[:i]) - i for i in range(len(counts))]
    stage_count = len(stages) - 1

    message, rhs, la, lb, moved, basis, chosen, params = call(
        functools.partial(setup_kernel, bases, total, subs),
        [
            f32_shape(message_rows(rows, rank, True), LANES),
            f32_shape(rows, size),
            bf16_shape(size, 16),
            bf16_shape(size, 80),
            f32_shape(8, size),
            bf16_shape(2 * size, rank),
            jax.ShapeDtypeStruct((slots, rank), jnp.int32),
            f32_shape(8, 128),
        ],
        [
            points,
            targets,
            leaf_skel,
            node_keep,
            jnp.reshape(lengthscales, (1, dims)),
            jnp.reshape(noise_var, (1, 1)),
        ],
        anywhere=range(6),
        pinned=range(5),
        scratch=[
            pltpu.VMEM((dims, size), F32),
            pltpu.VMEM((1, rank), jnp.int32),
            pltpu.VMEM(node_keep.shape, jnp.int32),
            pltpu.VMEM((1, dims), F32),
            pltpu.VMEM((1, 1), F32),
            pltpu.SemaphoreType.DMA((6,)),
        ],
        name="setup",
    )

    def tree_shapes(count):
        nodes = count - 1
        return [bf16_shape(nodes, 4 * rank, rank), bf16_shape(nodes, 2 * rank, rank)]

    first_width = size // BLOCK // 2 * BLOCK
    widths = [first_width, size - first_width]
    dense, near_parts = [], []

    def build_dense(start, width, tie):
        stacked, near = call(
            functools.partial(dense_kernel, start),
            [resident_shape(2 * size, width), f32_shape(rows, width)],
            [la, lb, moved, rhs, params, tie],
            cost=(6 * rows * size * width + 192 * size * width, size * width),
            name="dense",
        )
        dense.append(stacked)
        near_parts.append(near)

    trees, pending = [], []
    terms_all = []
    for i in range(stage_count):
        messages = gather(message, hops[i])
        extra = []
        if i == 0:
            build_dense(0, widths[0], params)
            extra = near_parts[:1]
        next_message, transfer, nodes = call(
            refs_of(lower_first_kernel, rows, counts[i], offsets[i]),
            [
                f32_shape(message_rows(rows, rank, True), LANES),
                tree_shapes(counts[i])[0],
                f32_shape(counts[i] - 1, 8, rank),
            ],
            messages + [params, chosen] + extra,
            name="lower_first",
        )
        pending.append((i, messages, transfer, nodes))
        message = next_message
    messages = gather(message, hops[-1])
    build_dense(widths[0], widths[1], message)
    (flipped,) = call(
        flip_kernel,
        [bf16_shape(2 * rank, size)],
        [basis, message],
        cost=(64 * size * rank, 0),
        name="flip",
    )
    basis = [basis, flipped]
    for i, arrived, transfer, nodes in pending:
        couple, terms = call(
            refs_of(lower_rest_kernel, rows, counts[i]),
            [tree_shapes(counts[i])[1], f32_shape(bases[i][1], rows, rank)],
            arrived + [params, transfer, nodes],
            cost=(48 * rank * rank * rank, rank * rank * counts[i]),
            name="lower_rest",
        )
        trees.append([transfer, couple])
        terms_all.append(terms)

    def build_upper(partial, extra):
        return call(
            refs_of(upper_build, rows, counts[-1], offsets[-1], partial),
            tree_shapes(counts[-1]),
            messages_first + [params, chosen] + extra,
            cost=None if partial else (48 * rank * rank * rank, rank * rank * counts[-1]),
            name="upper_build",
        )

    messages_first = messages
    upper = build_upper(True, [])

    state_shape = f32_shape(rows, 128)
    vector = f32_shape(rows, size)
    message_shape = f32_shape(message_rows(rows, rank, False), LANES)

    def lower_of(terms_all):
        return [a for terms, tree in zip(terms_all, trees) for a in (terms, tree[0])]

    def exchange(message, shadow=None):
        terms_all = []
        made = None
        for i in range(stage_count):
            messages = gather(message, hops[i])
            if i == 0 and shadow is not None:
                made = shadow()
            message, terms = call(
                refs_of(lower_kernel, rows, counts[i], True),
                [message_shape, f32_shape(bases[i][1], rows, rank)],
                messages + trees[i],
                name="lower",
            )
            terms_all.append(terms)
        return gather(message, hops[-1]) + terms_all, made

    fixed = (rows, counts[-1], stage_count)
    message, q, near, state = call(
        refs_of(first_kernel, *fixed, len(widths)),
        [message_shape, vector, vector, state_shape],
        messages + lower_of(terms_all) + upper + basis + dense + [params, rhs] + near_parts,
        resident=dense,
        name="first",
    )

    def compose():
        upper = build_upper(False, [state])
        pairs = [tree[0] for tree in trees + [upper]]
        path = call(
            refs_of(compose_kernel, counts),
            [bf16_shape(2 * (total - 1) * rank, rank)],
            pairs + [state],
            cost=(12 * rank * rank * rank, 0),
            name="compose",
        )
        return upper, path

    arrived, (upper, path) = exchange(message, compose)
    first_q = q
    message, r, q, near, state = call(
        refs_of(second_kernel, *fixed, len(widths)),
        [message_shape, vector, vector, vector, state_shape],
        arrived + upper + path + basis + dense + [params, rhs, q, near, state],
        resident=dense,
        name="second",
    )

    def update():
        return call(
            update_kernel,
            [vector, vector],
            [rhs, first_q, state],
            cost=(8 * rows * size, 0),
            name="update",
        )

    arrived, (x, d) = exchange(message, update)
    return tuple(
        call(
            refs_of(last_kernel, *fixed),
            [vector, vector],
            arrived + upper + path + basis + [x, r, d, q, near, state],
            copied=True,
            scratch=[
                pltpu.VMEM((rows, size), F32),
                pltpu.VMEM((rows, size), F32),
                pltpu.SemaphoreType.DMA((2,)),
            ],
            name="last",
        )
    )


def solution(mesh):
    in_specs = (
        P(None, ("parts", "leaf", "sub")),
        P(None, ("parts", "leaf", "sub")),
        P(("parts", "leaf", "sub"), None),
        P("parts", None),
        P("parts"),
        P("parts"),
    )
    out_specs = (P(None, ("parts", "leaf", "sub")), P(None, ("parts", "leaf", "sub")))
    return jax.shard_map(body, mesh=mesh, in_specs=in_specs, out_specs=out_specs, check_vma=False)
```
